128 devices in a mesh: row: 8 (over x, y_lo), col: 16 (over z, y_hi, core).
Axes of the slice: x: 4, y: 4 (y_hi: 2, y_lo: 2; y = y_hi * 2 + y_lo), z: 4, core: 2. Of those that a mesh axis runs over, the one named last changes fastest.
Arguments:
- amplitudes: float32 [16, 16, 256, 256], P('row', 'col'), may hold values from -6 to 6
- coulomb: bfloat16 [16, 16, 256, 256], P('row'), may hold values from -6 to 6
- inner_list: int32 [16, 16, 8], P('row', 'col'), may hold values from 0 to 15, as said below
- inner_count: int32 [16, 16], P('row', 'col'), may hold values from 4 to 8
- reader_list: int32 [16, 16, 8], P('row'), may hold values from 0 to 15, as said below
- reader_count: int32 [16, 16], P('row'), may hold values from 4 to 8
- virtual_energy: float32 [256], replicated, may hold values from 0.5 to 2.5
- occupied_energy: float32 [16], replicated, may hold values from -1.5 to -0.3
Outputs:
- new_amplitudes: float32 [16, 16, 256, 256], P('row', 'col')
The draws below stay inside these ranges and needn't reach their ends.
Inputs may be any that keep to these rules, and one draw needn't show every extreme that they name: `inner_list`: for each pair block the 8 entries are distinct orbitals; only the first inner_count of them are used. `reader_list`: for each pair block the 8 entries are distinct orbitals; only the first reader_count of them are used.
All inputs are finite; a program needn't handle non-finite values.
Results may differ from the reference program's by a relative error of at most 0.0015.
Values may be sent and summed in bfloat16 or wider, within the bound.
A program may use at most 64 MiB of HBM per device.

```python
import math
import jax
import jax.numpy as jnp
from jax import lax

V = 256
LMAX = 8
ITERS = 2
NO = 16


def distinct_lists(key):
    scores = jax.random.randint(key, (NO, NO, NO), 0, 2 ** 20) * NO + lax.broadcasted_iota(jnp.int32, (NO, NO, NO), 2)
    order = jnp.argsort(scores, axis=2)
    return order[:, :, :LMAX].astype(jnp.int32)


def listed_counts(key):
    counts = jax.random.randint(key, (NO, NO), LMAX // 2, LMAX + 1)
    return counts.at[0, 0].set(LMAX).astype(jnp.int32)


def draw_inner_list(key, part):
    return distinct_lists(jax.random.fold_in(key, 11))


def draw_inner_count(key, part):
    return listed_counts(jax.random.fold_in(key, 12))


def draw_reader_list(key, part):
    return distinct_lists(jax.random.fold_in(key, 13))


def draw_reader_count(key, part):
    return listed_counts(jax.random.fold_in(key, 14))


def shard_levels(stream_key, extent, split, smallest, largest):
    level = 1.0
    for axis_at, blocks in split:
        steps = jax.random.uniform(jax.random.fold_in(jax.random.fold_in(stream_key, 6), axis_at), (blocks,), jnp.float32, smallest / len(split), largest / len(split))
        level = level * jnp.repeat(jnp.exp(steps), extent[axis_at] // blocks).reshape((-1,) + (1,) * (len(extent) - 1 - axis_at))
    return level


def scatter_about(own_key, extent, scale, reach, cuts=(), kind=jnp.bfloat16):
    values = jax.random.normal(own_key, extent, jnp.float32) * scale
    if len(cuts) > 0:
        values = shard_levels(own_key, extent, cuts, -0.22, 0.18) * values
    return jnp.clip(values, min=-reach, max=reach).astype(kind)


def setup_inputs(seed: int = 0) -> dict:
    key_list = jax.random.split(jax.random.key(seed), 9)
    return {
        "amplitudes": scatter_about(key_list[0], (NO, NO, V, V), 1.0, 6.0, ((0, 8), (1, 16)), jnp.float32),
        "coulomb": scatter_about(key_list[1], (NO, NO, V, V), 1.0, 6.0, ((0, 8),)),
        "inner_list": draw_inner_list(jax.random.fold_in(key_list[8], 71), 0),
        "inner_count": draw_inner_count(jax.random.fold_in(key_list[8], 71), 0),
        "reader_list": draw_reader_list(jax.random.fold_in(key_list[8], 71), 0),
        "reader_count": draw_reader_count(jax.random.fold_in(key_list[8], 71), 0),
        "virtual_energy": jnp.clip(jnp.exp(jax.random.uniform(key_list[6], (V,), jnp.float32, math.log(0.5), math.log(2.5))), 0.5, 2.5),
        "occupied_energy": jnp.clip(jax.random.uniform(key_list[7], (NO,), jnp.float32, -1.5, -0.3), -1.5, -0.3),
    }


damping = 0.5
coupling = 0.03125


def reference(amplitudes, coulomb, inner_list, inner_count, reader_list, reader_count, virtual_energy, occupied_energy):
    slot_iota = jnp.arange(LMAX, dtype=jnp.int32)
    orbital_iota = jnp.arange(NO, dtype=jnp.int32)
    denominator = (virtual_energy[:, None] + virtual_energy[None, :])[None, None] - occupied_energy[:, None, None, None] - occupied_energy[None, :, None, None]
    amp_state = amplitudes
    for sweep_index in range(ITERS):
        amp_half = amp_state.astype(jnp.bfloat16)

        def coupled_row(orbital):
            listed = inner_list[orbital]
            weight = (slot_iota[None, :] < inner_count[orbital][:, None]).astype(jnp.float32)
            left_part = coulomb[orbital][listed].astype(jnp.float32)
            right_part = amp_half[listed, orbital_iota[:, None]].astype(jnp.float32)
            return jnp.einsum("jsab,jsbc,js->jac", left_part, right_part, weight)

        coupled = lax.map(coupled_row, orbital_iota).astype(jnp.bfloat16)

        def quad_row(orbital):
            listed = reader_list[orbital]
            weight = (slot_iota[None, :] < reader_count[orbital][:, None]).astype(jnp.float32)
            left_part = amp_half[orbital][listed].astype(jnp.float32)
            right_part = coupled[listed, orbital_iota[:, None]].astype(jnp.float32)
            return jnp.einsum("jsab,jsbc,js->jac", left_part, right_part, weight)

        quadratic = lax.map(quad_row, orbital_iota)
        mirror = jnp.transpose(coupled, (1, 0, 3, 2)).astype(jnp.float32)
        residual = coulomb.astype(jnp.float32) + coupling * (coupled.astype(jnp.float32) + mirror) + coupling * coupling * quadratic
        amp_state = damping * amp_state - residual / denominator
    return amp_state
```

```python
import functools

import jax
import jax.numpy as jnp
from jax import lax
from jax.experimental import pallas as pl
from jax.experimental.pallas import tpu as pltpu
from jax.sharding import PartitionSpec as P

ITERS = 2

damping = 0.5
coupling = 0.03125
MESH = pl.DeviceIdType.MESH
F32 = jnp.float32
BF16 = jnp.bfloat16

Y_P, Y_Q, Y_QM, Y_QP, Y_Q2A, Y_Q2B = range(6)
R_Q, R_P, R_QA, R_NA, R_NB, R_PA, R_NRA = range(6, 13)
L_Q, L_P, L_QB, L_NB, L_NA, L_PB, L_NRB = range(13, 20)
COL = 20
N_P, N_Q = 40, 41
ZR_O, ZR_H, ZR_OA, ZR_HA = range(42, 46)
ZL_O, ZL_H, ZL_OB, ZL_HB = range(46, 50)
S_O, S_H, S_M, S_P, S_HM, S_HP, S_2, S_H2 = range(50, 58)
M_0, M_1 = 58, 59
COUNT = 60


def kernel(
    nrow, ncol, slots, V,
    amp_ref, coul_ref, ilist_ref, icnt_ref, rlist_ref, rcnt_ref, virt_ref, occ_ref,
    out_ref,
    amps, coups, rows, coul, mirror, state, acc, base, inv, wlin, wquad,
    send_sem, recv_sem, load_sem,
):
    r = lax.axis_index("row")
    c = lax.axis_index("col")

    def flip(v, bit):
        return v + bit - 2 * bit * lax.rem(v // bit, 2)

    unit = 2 * V // 32
    pcut = 18 * unit
    part_p = pl.ds(0, pcut)
    part_q = pl.ds(pcut, 2 * V - pcut)
    pa, pb = pl.ds(0, pcut // 2), pl.ds(pcut // 2, pcut // 2)
    qhalf = (2 * V - pcut) // 2
    qa, qb = pl.ds(pcut, qhalf), pl.ds(pcut + qhalf, qhalf)
    whole = pl.ds(0, 2 * V)
    half_a, half_b = pl.ds(0, V), pl.ds(V, V)

    ry = flip(r, 1)
    rp, rm, r2 = lax.rem(r + 2, nrow), lax.rem(r + nrow - 2, nrow), lax.rem(r + 4, nrow)
    yp, ym, y2 = flip(rp, 1), flip(rm, 1), flip(r2, 1)
    ch, cs = flip(c, 2), flip(c, 1)
    cp, cm, c2 = lax.rem(c + 4, ncol), lax.rem(c + ncol - 4, ncol), lax.rem(c + 8, ncol)
    hp, hm, h2 = flip(cp, 2), flip(cm, 2), flip(c2, 2)
    to_y, to_right, to_left = (ry, c), (rp, c), (rm, c)
    to_n, to_zr, to_zl, to_s = (ry, ch), (r, cp), (r, cm), (r, cs)
    mrow = c // 2
    slot = lax.rem(c, 2)
    mcol = (2 * r, 2 * r + 1)
    mself = tuple(jnp.logical_and(mrow == r, mcol[a] == c) for a in range(2))

    loads = [
        pltpu.make_async_copy(amp_ref.at[a, 0], state.at[pl.ds(a * V, V)], load_sem.at[a])
        for a in range(2)
    ]
    for a in range(2):
        loads[a].start()
    coul_loads = [
        pltpu.make_async_copy(
            coul_ref.at[a], coul.at[:, pl.ds(a * V, V)], load_sem.at[2 + a]
        )
        for a in range(2)
    ]
    for a in range(2):
        coul_loads[a].start()

    barrier = pltpu.get_barrier_semaphore()
    for dev in (to_y, to_right, to_left, to_n, to_zr, to_zl, to_s):
        pl.semaphore_signal(barrier, inc=1, device_id=dev, device_id_type=MESH)
    for a in range(2):
        @pl.when(jnp.logical_not(mself[a]))
        def _():
            pl.semaphore_signal(barrier, inc=1, device_id=(mrow, mcol[a]), device_id_type=MESH)
    on_diagonal = mrow == r

    @pl.when(on_diagonal)
    def _():
        pl.semaphore_wait(barrier, 8)

    @pl.when(jnp.logical_not(on_diagonal))
    def _():
        pl.semaphore_wait(barrier, 9)

    for a in range(2):
        loads[a].wait()

    def sweep(s, carry):
        def message(src, dst, key, dev, recv_key=None):
            return pltpu.make_async_remote_copy(
                src_ref=src, dst_ref=dst, send_sem=send_sem.at[s, key],
                recv_sem=recv_sem.at[s, key if recv_key is None else recv_key],
                device_id=dev, device_id_type=MESH,
            )

        def send(ref, key, dev):
            message(ref, ref, key, dev).start()

        def arrived(ref, key):
            message(ref, ref, key, to_y).wait_recv()

        def consume(left, weight, right, source, first=False):
            for b in range(2):
                orbital = 2 * source + b
                block = right[s, source, b * V:(b + 1) * V, :]
                for a in range(2):
                    at = slice(a * V, (a + 1) * V)
                    part = jnp.dot(left(orbital, a), block, preferred_element_type=F32)
                    part = part * weight[a, orbital]
                    if first and b == 0:
                        acc[at, :] = part
                    else:
                        acc[at, :] += part

        def open_gather(buf, o):
            own = buf.at[s, r]
            send(own.at[part_p], o + Y_P, to_y)
            send(own.at[part_q], o + R_Q, to_right)
            send(own.at[part_q], o + L_Q, to_left)
            send(own.at[part_q], o + Y_Q, to_y)
            send(own.at[part_p], o + R_P, to_right)
            send(own.at[part_p], o + L_P, to_left)

        def relay_q(buf, o):
            arrived(buf.at[s, rm, part_q], o + R_Q)
            send(buf.at[s, rm, qa], o + R_QA, to_right)
            send(buf.at[s, rm, part_q], o + Y_QM, to_y)
            arrived(buf.at[s, rp, part_q], o + L_Q)
            send(buf.at[s, rp, qb], o + L_QB, to_left)
            send(buf.at[s, rp, part_q], o + Y_QP, to_y)

        def relay_n(buf, o):
            arrived(buf.at[s, ry, part_p], o + Y_P)
            send(buf.at[s, ry, pa], o + R_NA, to_right)
            send(buf.at[s, ry, pb], o + L_NB, to_left)
            send(buf.at[s, ry, pb], o + R_NB, to_right)
            send(buf.at[s, ry, pa], o + L_NA, to_left)

        def relay_p(buf, o):
            arrived(buf.at[s, rm, part_p], o + R_P)
            send(buf.at[s, rm, pa], o + R_PA, to_right)
            arrived(buf.at[s, rp, part_p], o + L_P)
            send(buf.at[s, rp, pb], o + L_PB, to_left)

        def relay_q2(buf, o):
            arrived(buf.at[s, r2, qa], o + R_QA)
            send(buf.at[s, r2, qa], o + Y_Q2A, to_y)
            arrived(buf.at[s, r2, qb], o + L_QB)
            send(buf.at[s, r2, qb], o + Y_Q2B, to_y)

        def relay_nn(buf, o):
            arrived(buf.at[s, ym, pa], o + R_NA)
            send(buf.at[s, ym, pa], o + R_NRA, to_right)
            arrived(buf.at[s, yp, pb], o + L_NB)
            send(buf.at[s, yp, pb], o + L_NRB, to_left)
            arrived(buf.at[s, ym, pb], o + R_NB)
            arrived(buf.at[s, yp, pa], o + L_NA)

        def lin_left(orbital, a):
            return coul[orbital, a * V:(a + 1) * V, :]

        def quad_left(orbital, a):
            return rows[s, orbital, a * V:(a + 1) * V, :]

        start = state[...].astype(BF16)
        amps[s, r] = start
        rows[s, c] = start
        open_gather(amps, 0)
        send(rows.at[s, c], ZR_O, to_zr)
        send(rows.at[s, c], ZL_O, to_zl)
        send(rows.at[s, c], S_O, to_s)

        @pl.when(s == 0)
        def _():
            for weight, entries, count in (
                (wlin, lambda a, t: ilist_ref[a, 0, t], lambda a: icnt_ref[a, 0]),
                (wquad, lambda a, t: rlist_ref[a, c, t], lambda a: rcnt_ref[a, c]),
            ):
                for a in range(2):
                    used = count(a)
                    listed = [jnp.where(t < used, entries(a, t), -1) for t in range(slots)]
                    for orbital in range(ncol):
                        hit = listed[0] == orbital
                        for t in range(1, slots):
                            hit = jnp.logical_or(hit, listed[t] == orbital)
                        weight[a, orbital] = jnp.where(hit, 1.0, 0.0).astype(F32)
            across = jnp.broadcast_to(virt_ref[...], (V, V))
            pair = across + across.T
            for a in range(2):
                inv[a * V:(a + 1) * V, :] = 1.0 / (pair - occ_ref[2 * r + a] - occ_ref[c])
            for a in range(2):
                coul_loads[a].wait()

        consume(lin_left, wlin, amps, r, first=True)
        relay_q(amps, 0)
        relay_n(amps, 0)
        message(amps.at[s, ry, part_p], rows.at[s, c, part_p], N_P, to_n).start()
        relay_p(amps, 0)
        arrived(amps.at[s, ry, part_q], Y_Q)
        message(amps.at[s, ry, part_q], rows.at[s, c, part_q], N_Q, to_n).start()
        arrived(rows.at[s, cm], ZR_O)
        send(rows.at[s, cm, half_a], ZR_OA, to_zr)
        send(rows.at[s, cm], S_M, to_s)
        arrived(rows.at[s, cp], ZL_O)
        send(rows.at[s, cp, half_b], ZL_OB, to_zl)
        send(rows.at[s, cp], S_P, to_s)
        consume(lin_left, wlin, amps, rm)
        relay_q2(amps, 0)
        consume(lin_left, wlin, amps, rp)
        consume(lin_left, wlin, amps, ry)
        relay_nn(amps, 0)
        arrived(rows.at[s, ch, part_p], N_P)
        arrived(rows.at[s, ch, part_q], N_Q)
        send(rows.at[s, ch], ZR_H, to_zr)
        send(rows.at[s, ch], ZL_H, to_zl)
        send(rows.at[s, ch], S_H, to_s)
        arrived(amps.at[s, ym, part_q], Y_QM)
        consume(lin_left, wlin, amps, ym)
        arrived(amps.at[s, yp, part_q], Y_QP)
        consume(lin_left, wlin, amps, yp)
        arrived(amps.at[s, r2, pa], R_PA)
        arrived(amps.at[s, r2, pb], L_PB)
        consume(lin_left, wlin, amps, r2)
        arrived(rows.at[s, c2, half_a], ZR_OA)
        arrived(rows.at[s, c2, half_b], ZL_OB)
        send(rows.at[s, c2], S_2, to_s)
        arrived(amps.at[s, y2, qa], Y_Q2A)
        arrived(amps.at[s, y2, qb], Y_Q2B)
        arrived(amps.at[s, y2, pa], R_NRA)
        arrived(amps.at[s, y2, pb], L_NRB)
        consume(lin_left, wlin, amps, y2)

        coups[s, r] = acc[...].astype(BF16)
        open_gather(coups, COL)
        for a in range(2):
            block = coups.at[s, r, pl.ds(a * V, V)]

            @pl.when(jnp.logical_not(mself[a]))
            def _():
                message(
                    block, mirror.at[s, slot], M_0 + a, (mrow, mcol[a]), M_0 + slot
                ).start()

            @pl.when(mself[a])
            def _():
                mirror[s, a] = coups[s, r, a * V:(a + 1) * V, :]

        for a in range(2):
            at = slice(a * V, (a + 1) * V)
            linear = coul[c, at, :].astype(F32) + coupling * coups[s, r, at, :].astype(F32)
            base[at, :] = damping * state[at, :] - linear * inv[at, :]
        relay_q(coups, COL)
        relay_n(coups, COL)
        arrived(rows.at[s, hm], ZR_H)
        send(rows.at[s, hm, half_a], ZR_HA, to_zr)
        send(rows.at[s, hm], S_HM, to_s)
        arrived(rows.at[s, hp], ZL_H)
        send(rows.at[s, hp, half_b], ZL_HB, to_zl)
        send(rows.at[s, hp], S_HP, to_s)
        relay_p(coups, COL)
        relay_q2(coups, COL)
        arrived(coups.at[s, ry, part_q], COL + Y_Q)
        arrived(rows.at[s, h2, half_a], ZR_HA)
        arrived(rows.at[s, h2, half_b], ZL_HB)
        send(rows.at[s, h2], S_H2, to_s)
        for own, key in (
            (c, S_O), (ch, S_H), (cm, S_M), (cp, S_P),
            (hm, S_HM), (hp, S_HP), (c2, S_2), (h2, S_H2),
        ):
            arrived(rows.at[s, flip(own, 1)], key)
        consume(quad_left, wquad, coups, r, first=True)
        consume(quad_left, wquad, coups, rm)
        relay_nn(coups, COL)
        consume(quad_left, wquad, coups, rp)
        consume(quad_left, wquad, coups, ry)
        arrived(coups.at[s, ym, part_q], COL + Y_QM)
        consume(quad_left, wquad, coups, ym)
        arrived(coups.at[s, yp, part_q], COL + Y_QP)
        consume(quad_left, wquad, coups, yp)
        arrived(coups.at[s, r2, pa], COL + R_PA)
        arrived(coups.at[s, r2, pb], COL + L_PB)
        consume(quad_left, wquad, coups, r2)
        for a in range(2):
            @pl.when(jnp.logical_not(mself[a]))
            def _():
                arrived(mirror.at[s, a], M_0 + a)

            at = slice(a * V, (a + 1) * V)
            flipped = mirror[s, a].astype(F32).T
            base[at, :] -= coupling * flipped * inv[at, :]
        arrived(coups.at[s, y2, qa], COL + Y_Q2A)
        arrived(coups.at[s, y2, qb], COL + Y_Q2B)
        arrived(coups.at[s, y2, pa], COL + R_NRA)
        arrived(coups.at[s, y2, pb], COL + L_NRB)
        consume(quad_left, wquad, coups, y2)
        state[...] = base[...] - (coupling * coupling) * acc[...] * inv[...]
        return carry

    lax.fori_loop(0, ITERS, sweep, 0)

    stores = [
        pltpu.make_async_copy(state.at[pl.ds(a * V, V)], out_ref.at[a, 0], load_sem.at[a])
        for a in range(2)
    ]
    for a in range(2):
        stores[a].start()
    sizes = {}
    for o in (0, COL):
        for keys, ref in (
            ((Y_P, R_P, L_P), amps.at[0, r, part_p]),
            ((Y_Q, Y_QM, Y_QP, R_Q, L_Q), amps.at[0, r, part_q]),
            ((Y_Q2A, Y_Q2B, R_QA, L_QB), amps.at[0, r, qa]),
            ((R_NA, R_NB, R_PA, R_NRA, L_NB, L_NA, L_PB, L_NRB), amps.at[0, r, pa]),
        ):
            for key in keys:
                sizes[o + key] = ref
    sizes[N_P], sizes[N_Q] = amps.at[0, r, part_p], amps.at[0, r, part_q]
    for key in (ZR_O, ZR_H, ZL_O, ZL_H, *range(S_O, S_H2 + 1)):
        sizes[key] = rows.at[0, c]
    for key in (ZR_OA, ZR_HA, ZL_OB, ZL_HB):
        sizes[key] = rows.at[0, c, half_a]

    def drain(s, carry):
        def sent(ref, key):
            pltpu.make_async_remote_copy(
                src_ref=ref, dst_ref=ref, send_sem=send_sem.at[s, key],
                recv_sem=recv_sem.at[s, key], device_id=to_y, device_id_type=MESH,
            ).wait_send()

        for key, ref in sizes.items():
            sent(ref, key)
        for a in range(2):
            @pl.when(jnp.logical_not(mself[a]))
            def _():
                sent(mirror.at[0, a], M_0 + a)
        return carry

    lax.fori_loop(0, ITERS, drain, 0)
    for a in range(2):
        stores[a].wait()


def on_device(
    amplitudes,
    coulomb,
    inner_list,
    inner_count,
    reader_list,
    reader_count,
    virtual_energy,
    occupied_energy,
    *,
    nrow,
    ncol,
):
    V = amplitudes.shape[2]
    slots = inner_list.shape[2]
    hbm = pl.BlockSpec(memory_space=pl.ANY)
    smem = pl.BlockSpec(memory_space=pltpu.SMEM)
    vmem = pl.BlockSpec(memory_space=pltpu.VMEM)
    return pl.pallas_call(
        functools.partial(kernel, nrow, ncol, slots, V),
        out_shape=jax.ShapeDtypeStruct(amplitudes.shape, F32),
        in_specs=[hbm, hbm, smem, smem, smem, smem, vmem, smem],
        out_specs=hbm,
        scratch_shapes=[
            pltpu.VMEM((ITERS, nrow, 2 * V, V), BF16),
            pltpu.VMEM((ITERS, nrow, 2 * V, V), BF16),
            pltpu.VMEM((ITERS, ncol, 2 * V, V), BF16),
            pltpu.VMEM((ncol, 2 * V, V), BF16),
            pltpu.VMEM((ITERS, 2, V, V), BF16),
            pltpu.VMEM((2 * V, V), F32),
            pltpu.VMEM((2 * V, V), F32),
            pltpu.VMEM((2 * V, V), F32),
            pltpu.VMEM((2 * V, V), F32),
            pltpu.SMEM((2, ncol), F32),
            pltpu.SMEM((2, ncol), F32),
            pltpu.SemaphoreType.DMA((ITERS, COUNT)),
            pltpu.SemaphoreType.DMA((ITERS, COUNT)),
            pltpu.SemaphoreType.DMA((4,)),
        ],
        compiler_params=pltpu.CompilerParams(
            collective_id=0, has_side_effects=True, vmem_limit_bytes=48 * 1024 * 1024
        ),
        name="sweeps",
    )(
        amplitudes,
        coulomb,
        inner_list,
        inner_count,
        reader_list,
        reader_count,
        virtual_energy.reshape(1, V),
        occupied_energy,
    )


def solution(mesh):
    return jax.shard_map(
        functools.partial(on_device, nrow=mesh.shape["row"], ncol=mesh.shape["col"]),
        mesh=mesh,
        in_specs=(
            P("row", "col", None, None),
            P("row", None, None, None),
            P("row", "col", None),
            P("row", "col"),
            P("row", None, None),
            P("row", None),
            P(),
            P(),
        ),
        out_specs=P("row", "col", None, None),
        check_vma=False,
    )
```

```python
import functools

import jax
import jax.numpy as jnp
from jax import lax
from jax.experimental import pallas as pl
from jax.experimental.pallas import tpu as pltpu
from jax.sharding import PartitionSpec as P

ITERS = 2

damping = 0.5
coupling = 0.03125
MESH = pl.DeviceIdType.MESH
F32 = jnp.float32
BF16 = jnp.bfloat16

Y_P, Y_Q, Y_QM, Y_QP, Y_Q2A, Y_Q2B = range(6)
R_Q, R_P, R_QA, R_NA, R_NB, R_PA, R_NRA = range(6, 13)
L_Q, L_P, L_QB, L_NB, L_NA, L_PB, L_NRB = range(13, 20)
COL = 20
N_P, N_Q = 40, 41
ZR_O, ZR_H, ZR_OA, ZR_HA = range(42, 46)
ZL_O, ZL_H, ZL_OB, ZL_HB = range(46, 50)
S_O, S_H, S_M, S_P, S_HM, S_HP, S_2, S_H2 = range(50, 58)
M_0, M_1, X_0, X_1 = range(58, 62)
COUNT = 62
LINEAR_CUT, COUPLED_CUT = 18, 16


def kernel(
    nrow, ncol, slots, V,
    amp_ref, coul_ref, ilist_ref, icnt_ref, rlist_ref, rcnt_ref, virt_ref, occ_ref,
    out_ref,
    amps, coups, rows, coul, mirror, transit, state, acc, base, inv, wlin, wquad,
    ilist, icnt, rlist, rcnt, virt, occ,
    send_sem, recv_sem, load_sem,
):
    r = lax.axis_index("row")
    c = lax.axis_index("col")

    def flip(v, bit):
        return v + bit - 2 * bit * lax.rem(v // bit, 2)

    unit = 2 * V // 32

    def cut(parts):
        first, rest = parts * unit, (32 - parts) * unit
        return dict(
            p=pl.ds(0, first), pa=pl.ds(0, first // 2), pb=pl.ds(first // 2, first // 2),
            q=pl.ds(first, rest), qa=pl.ds(first, rest // 2),
            qb=pl.ds(first + rest // 2, rest // 2),
        )

    lin, quad = cut(LINEAR_CUT), cut(COUPLED_CUT)
    cuts = {0: lin, COL: quad}
    half_a, half_b = pl.ds(0, V), pl.ds(V, V)

    ry = flip(r, 1)
    rp, rm, r2 = lax.rem(r + 2, nrow), lax.rem(r + nrow - 2, nrow), lax.rem(r + 4, nrow)
    yp, ym, y2 = flip(rp, 1), flip(rm, 1), flip(r2, 1)
    ch, cs = flip(c, 2), flip(c, 1)
    cp, cm, c2 = lax.rem(c + 4, ncol), lax.rem(c + ncol - 4, ncol), lax.rem(c + 8, ncol)
    hp, hm, h2 = flip(cp, 2), flip(cm, 2), flip(c2, 2)
    to_y, to_right, to_left = (ry, c), (rp, c), (rm, c)
    to_n, to_zr, to_zl, to_s = (ry, ch), (r, cp), (r, cm), (r, cs)
    nx = nrow // 2
    x, lo = r // 2, lax.rem(r, 2)
    z, hi, core = c // 4, lax.rem(c // 2, 2), lax.rem(c, 2)
    ahead = lax.rem(z - x + nx, nx)

    def place(px, pz, plo, phi, pcore):
        return (
            2 * lax.rem(px + nx, nx) + plo, 4 * lax.rem(pz + nx, nx) + 2 * phi + pcore
        )

    step = 2 - ahead
    diagonal = ahead == 0
    opposite = ahead == 2
    beside = jnp.logical_or(ahead == 1, ahead == 3)
    mself = tuple(
        jnp.logical_and(diagonal, jnp.logical_and(lo == hi, core == a)) for a in range(2)
    )
    mout = tuple(jnp.logical_and(diagonal, jnp.logical_not(mself[a])) for a in range(2))

    loads = [
        pltpu.make_async_copy(amp_ref.at[a, 0], state.at[pl.ds(a * V, V)], load_sem.at[a])
        for a in range(2)
    ]
    for a in range(2):
        loads[a].start()
    coul_loads = [
        pltpu.make_async_copy(
            coul_ref.at[a], coul.at[:, pl.ds(a * V, V)], load_sem.at[2 + a]
        )
        for a in range(2)
    ]
    for a in range(2):
        coul_loads[a].start()
    small_loads = [
        pltpu.make_async_copy(src, dst, load_sem.at[4 + at])
        for at, (src, dst) in enumerate((
            (ilist_ref, ilist), (icnt_ref, icnt), (rlist_ref, rlist), (rcnt_ref, rcnt),
            (virt_ref, virt), (occ_ref, occ),
        ))
    ]
    for load in small_loads:
        load.start()

    barrier = pltpu.get_barrier_semaphore()
    for dev in (to_y, to_right, to_left, to_n, to_zr, to_zl, to_s):
        pl.semaphore_signal(barrier, inc=1, device_id=dev, device_id_type=MESH)

    def greet(condition, *devices):
        @pl.when(condition)
        def _():
            for dev in devices:
                pl.semaphore_signal(barrier, inc=1, device_id=dev, device_id_type=MESH)

    greet(diagonal, place(x, z + 1, hi, lo, core), place(x, z - 1, hi, lo, core))
    for a in range(2):
        greet(mout[a], place(x, z, hi, lo, a))
        greet(jnp.logical_and(beside, core == 0), place(z, x, hi, lo, a))
        greet(jnp.logical_and(beside, core == 1), place(z, z, lo, hi, a))
        greet(jnp.logical_and(opposite, core == 0), place(x - 1, z, lo, hi, a))
        greet(jnp.logical_and(opposite, core == 1), place(x + 1, z, lo, hi, a))
    greet(beside, place(x - step, z, lo, hi, core), place(x, z + 2, hi, lo, core))
    for condition, count in (
        (jnp.logical_or(beside, jnp.logical_and(diagonal, lo != hi)), 11),
        (jnp.logical_and(diagonal, lo == hi), 10),
        (opposite, 9),
    ):
        @pl.when(condition)
        def _():
            pl.semaphore_wait(barrier, count)

    for a in range(2):
        loads[a].wait()

    def sweep(s, carry):
        def message(src, dst, key, dev, recv_key=None):
            return pltpu.make_async_remote_copy(
                src_ref=src, dst_ref=dst, send_sem=send_sem.at[s, key],
                recv_sem=recv_sem.at[s, key if recv_key is None else recv_key],
                device_id=dev, device_id_type=MESH,
            )

        def send(ref, key, dev):
            message(ref, ref, key, dev).start()

        def arrived(ref, key):
            message(ref, ref, key, to_y).wait_recv()

        def consume(left, weight, right, source, first=False):
            for b in range(2):
                orbital = 2 * source + b
                block = right[s, source, b * V:(b + 1) * V, :]
                for a in range(2):
                    at = slice(a * V, (a + 1) * V)
                    part = jnp.dot(left(orbital, a), block, preferred_element_type=F32)
                    part = part * weight[a, orbital]
                    if first and b == 0:
                        acc[at, :] = part
                    else:
                        acc[at, :] += part

        def open_gather(buf, o):
            k = cuts[o]
            own = buf.at[s, r]
            send(own.at[k["p"]], o + Y_P, to_y)
            send(own.at[k["q"]], o + R_Q, to_right)
            send(own.at[k["q"]], o + L_Q, to_left)
            send(own.at[k["q"]], o + Y_Q, to_y)
            send(own.at[k["p"]], o + R_P, to_right)
            send(own.at[k["p"]], o + L_P, to_left)

        def relay_q(buf, o):
            k = cuts[o]
            arrived(buf.at[s, rm, k["q"]], o + R_Q)
            send(buf.at[s, rm, k["qa"]], o + R_QA, to_right)
            send(buf.at[s, rm, k["q"]], o + Y_QM, to_y)
            arrived(buf.at[s, rp, k["q"]], o + L_Q)
            send(buf.at[s, rp, k["qb"]], o + L_QB, to_left)
            send(buf.at[s, rp, k["q"]], o + Y_QP, to_y)

        def relay_n(buf, o):
            k = cuts[o]
            arrived(buf.at[s, ry, k["p"]], o + Y_P)
            send(buf.at[s, ry, k["pa"]], o + R_NA, to_right)
            send(buf.at[s, ry, k["pb"]], o + L_NB, to_left)
            send(buf.at[s, ry, k["pb"]], o + R_NB, to_right)
            send(buf.at[s, ry, k["pa"]], o + L_NA, to_left)

        def relay_p(buf, o):
            k = cuts[o]
            arrived(buf.at[s, rm, k["p"]], o + R_P)
            send(buf.at[s, rm, k["pa"]], o + R_PA, to_right)
            arrived(buf.at[s, rp, k["p"]], o + L_P)
            send(buf.at[s, rp, k["pb"]], o + L_PB, to_left)

        def relay_q2(buf, o):
            k = cuts[o]
            arrived(buf.at[s, r2, k["qa"]], o + R_QA)
            send(buf.at[s, r2, k["qa"]], o + Y_Q2A, to_y)
            arrived(buf.at[s, r2, k["qb"]], o + L_QB)
            send(buf.at[s, r2, k["qb"]], o + Y_Q2B, to_y)

        def relay_nn(buf, o):
            k = cuts[o]
            arrived(buf.at[s, ym, k["pa"]], o + R_NA)
            send(buf.at[s, ym, k["pa"]], o + R_NRA, to_right)
            arrived(buf.at[s, yp, k["pb"]], o + L_NB)
            send(buf.at[s, yp, k["pb"]], o + L_NRB, to_left)
            arrived(buf.at[s, ym, k["pb"]], o + R_NB)
            arrived(buf.at[s, yp, k["pa"]], o + L_NA)

        def lin_left(orbital, a):
            return coul[orbital, a * V:(a + 1) * V, :]

        def quad_left(orbital, a):
            return rows[s, orbital, a * V:(a + 1) * V, :]

        start = state[...].astype(BF16)
        amps[s, r] = start
        rows[s, c] = start
        open_gather(amps, 0)
        send(rows.at[s, c], ZR_O, to_zr)
        send(rows.at[s, c], ZL_O, to_zl)
        send(rows.at[s, c], S_O, to_s)

        @pl.when(s == 0)
        def _():
            for load in small_loads:
                load.wait()
            for weight, entries, count in (
                (wlin, lambda a, t: ilist[a, 0, t], lambda a: icnt[0, a]),
                (wquad, lambda a, t: rlist[a, t, c], lambda a: rcnt[a, c]),
            ):
                for a in range(2):
                    used = count(a)
                    listed = [jnp.where(t < used, entries(a, t), -1) for t in range(slots)]
                    for orbital in range(ncol):
                        hit = listed[0] == orbital
                        for t in range(1, slots):
                            hit = jnp.logical_or(hit, listed[t] == orbital)
                        weight[a, orbital] = jnp.where(hit, 1.0, 0.0).astype(F32)
            across = jnp.broadcast_to(virt[...], (V, V))
            pair = across + across.T
            for a in range(2):
                inv[a * V:(a + 1) * V, :] = 1.0 / (pair - occ[2 * r + a] - occ[c])
            for a in range(2):
                coul_loads[a].wait()

        consume(lin_left, wlin, amps, r, first=True)
        relay_q(amps, 0)
        relay_n(amps, 0)
        message(amps.at[s, ry, lin["p"]], rows.at[s, c, lin["p"]], N_P, to_n).start()
        relay_p(amps, 0)
        arrived(amps.at[s, ry, lin["q"]], Y_Q)
        message(amps.at[s, ry, lin["q"]], rows.at[s, c, lin["q"]], N_Q, to_n).start()
        arrived(rows.at[s, cm], ZR_O)
        send(rows.at[s, cm, half_a], ZR_OA, to_zr)
        send(rows.at[s, cm], S_M, to_s)
        arrived(rows.at[s, cp], ZL_O)
        send(rows.at[s, cp, half_b], ZL_OB, to_zl)
        send(rows.at[s, cp], S_P, to_s)
        consume(lin_left, wlin, amps, rm)
        relay_q2(amps, 0)
        consume(lin_left, wlin, amps, rp)
        consume(lin_left, wlin, amps, ry)
        relay_nn(amps, 0)
        arrived(rows.at[s, ch, lin["p"]], N_P)
        arrived(rows.at[s, ch, lin["q"]], N_Q)
        send(rows.at[s, ch], ZR_H, to_zr)
        send(rows.at[s, ch], ZL_H, to_zl)
        send(rows.at[s, ch], S_H, to_s)
        arrived(amps.at[s, ym, lin["q"]], Y_QM)
        consume(lin_left, wlin, amps, ym)
        arrived(amps.at[s, yp, lin["q"]], Y_QP)
        consume(lin_left, wlin, amps, yp)
        arrived(amps.at[s, r2, lin["pa"]], R_PA)
        arrived(amps.at[s, r2, lin["pb"]], L_PB)
        consume(lin_left, wlin, amps, r2)
        arrived(rows.at[s, c2, half_a], ZR_OA)
        arrived(rows.at[s, c2, half_b], ZL_OB)
        send(rows.at[s, c2], S_2, to_s)
        arrived(amps.at[s, y2, lin["qa"]], Y_Q2A)
        arrived(amps.at[s, y2, lin["qb"]], Y_Q2B)
        arrived(amps.at[s, y2, lin["pa"]], R_NRA)
        arrived(amps.at[s, y2, lin["pb"]], L_NRB)
        consume(lin_left, wlin, amps, y2)

        coups[s, r] = acc[...].astype(BF16)
        block = [coups.at[s, r, half_a], coups.at[s, r, half_b]]
        final = (mirror.at[s, core], M_0 + core)

        def forward(src, key, target, dev):
            message(src, target[0], key, dev, target[1]).start()

        @pl.when(opposite)
        def _():
            first = (transit.at[s, 0], X_0)
            forward(block[0], M_0, first, place(x + 1, z, lo, hi, core))
            forward(block[1], M_1, first, place(x - 1, z, lo, hi, core))

        open_gather(coups, COL)

        @pl.when(beside)
        def _():
            crossing = ahead // 2
            forward(
                block[1], M_1, (transit.at[s, crossing], X_0 + crossing),
                place(x, x, hi, lo, core),
            )
            forward(block[0], M_0, final, place(z, x, hi, lo, 0))

        for a in range(2):
            @pl.when(mout[a])
            def _():
                forward(block[a], M_0 + a, final, place(x, z, hi, lo, a))

            @pl.when(mself[a])
            def _():
                mirror[s, a] = coups[s, r, a * V:(a + 1) * V, :]

        for a in range(2):
            at = slice(a * V, (a + 1) * V)
            linear = coul[c, at, :].astype(F32) + coupling * coups[s, r, at, :].astype(F32)
            base[at, :] = damping * state[at, :] - linear * inv[at, :]
        relay_q(coups, COL)
        relay_n(coups, COL)

        @pl.when(diagonal)
        def _():
            for at, px in ((0, x + 1), (1, x - 1)):
                arrived(transit.at[s, at], X_0 + at)
                forward(transit.at[s, at], X_0 + at, final, place(px, z, lo, hi, 1))

        @pl.when(beside)
        def _():
            arrived(transit.at[s, 0], X_0)
            forward(
                transit.at[s, 0], X_0, (transit.at[s, 1], X_1), place(x, z + 2, hi, lo, core)
            )

        arrived(rows.at[s, hm], ZR_H)
        send(rows.at[s, hm, half_a], ZR_HA, to_zr)
        send(rows.at[s, hm], S_HM, to_s)
        arrived(rows.at[s, hp], ZL_H)
        send(rows.at[s, hp, half_b], ZL_HB, to_zl)
        send(rows.at[s, hp], S_HP, to_s)
        relay_p(coups, COL)
        relay_q2(coups, COL)

        @pl.when(beside)
        def _():
            arrived(transit.at[s, 1], X_1)
            forward(transit.at[s, 1], X_1, final, place(x - step, z, lo, hi, ahead % 3))

        arrived(coups.at[s, ry, quad["q"]], COL + Y_Q)
        arrived(rows.at[s, h2, half_a], ZR_HA)
        arrived(rows.at[s, h2, half_b], ZL_HB)
        send(rows.at[s, h2], S_H2, to_s)
        for own, key in (
            (c, S_O), (ch, S_H), (cm, S_M), (cp, S_P),
            (hm, S_HM), (hp, S_HP), (c2, S_2), (h2, S_H2),
        ):
            arrived(rows.at[s, flip(own, 1)], key)
        consume(quad_left, wquad, coups, r, first=True)
        consume(quad_left, wquad, coups, rm)
        relay_nn(coups, COL)
        consume(quad_left, wquad, coups, rp)
        consume(quad_left, wquad, coups, ry)
        arrived(coups.at[s, ym, quad["q"]], COL + Y_QM)
        consume(quad_left, wquad, coups, ym)
        arrived(coups.at[s, yp, quad["q"]], COL + Y_QP)
        consume(quad_left, wquad, coups, yp)
        arrived(coups.at[s, r2, quad["pa"]], COL + R_PA)
        arrived(coups.at[s, r2, quad["pb"]], COL + L_PB)
        consume(quad_left, wquad, coups, r2)
        for a in range(2):
            @pl.when(jnp.logical_not(mself[a]))
            def _():
                arrived(mirror.at[s, a], M_0 + a)

            at = slice(a * V, (a + 1) * V)
            flipped = mirror[s, a].astype(F32).T
            base[at, :] -= coupling * flipped * inv[at, :]
        arrived(coups.at[s, y2, quad["qa"]], COL + Y_Q2A)
        arrived(coups.at[s, y2, quad["qb"]], COL + Y_Q2B)
        arrived(coups.at[s, y2, quad["pa"]], COL + R_NRA)
        arrived(coups.at[s, y2, quad["pb"]], COL + L_NRB)
        consume(quad_left, wquad, coups, y2)
        state[...] = base[...] - (coupling * coupling) * acc[...] * inv[...]
        return carry

    lax.fori_loop(0, ITERS, sweep, 0)
    for a in range(2):
        out_ref[a, 0] = state[a * V:(a + 1) * V, :]
    sizes = {}
    for o, k in cuts.items():
        for keys, part in (
            ((Y_P, R_P, L_P), "p"),
            ((Y_Q, Y_QM, Y_QP, R_Q, L_Q), "q"),
            ((Y_Q2A, Y_Q2B, R_QA, L_QB), "qa"),
            ((R_NA, R_NB, R_PA, R_NRA, L_NB, L_NA, L_PB, L_NRB), "pa"),
        ):
            for key in keys:
                sizes[o + key] = amps.at[0, r, k[part]]
    sizes[N_P], sizes[N_Q] = amps.at[0, r, lin["p"]], amps.at[0, r, lin["q"]]
    for key in (ZR_O, ZR_H, ZL_O, ZL_H, *range(S_O, S_H2 + 1)):
        sizes[key] = rows.at[0, c]
    for key in (ZR_OA, ZR_HA, ZL_OB, ZL_HB):
        sizes[key] = rows.at[0, c, half_a]

    def drain(s, carry):
        def sent(ref, key):
            pltpu.make_async_remote_copy(
                src_ref=ref, dst_ref=ref, send_sem=send_sem.at[s, key],
                recv_sem=recv_sem.at[s, key], device_id=to_y, device_id_type=MESH,
            ).wait_send()

        for key, ref in sizes.items():
            sent(ref, key)
        for a in range(2):
            @pl.when(jnp.logical_not(mself[a]))
            def _():
                sent(mirror.at[0, a], M_0 + a)

        @pl.when(jnp.logical_not(opposite))
        def _():
            for a in range(2):
                sent(transit.at[0, a], X_0 + a)

        return carry

    lax.fori_loop(0, ITERS, drain, 0)


def on_device(
    amplitudes,
    coulomb,
    inner_list,
    inner_count,
    reader_list,
    reader_count,
    virtual_energy,
    occupied_energy,
    *,
    nrow,
    ncol,
):
    V = amplitudes.shape[2]
    slots = inner_list.shape[2]
    hbm = pl.BlockSpec(memory_space=pltpu.HBM)
    vmem = pl.BlockSpec(memory_space=pltpu.VMEM)
    return pl.pallas_call(
        functools.partial(kernel, nrow, ncol, slots, V),
        out_shape=jax.ShapeDtypeStruct(amplitudes.shape, F32),
        in_specs=[hbm] * 8,
        out_specs=vmem,
        scratch_shapes=[
            pltpu.VMEM((ITERS, nrow, 2 * V, V), BF16),
            pltpu.VMEM((ITERS, nrow, 2 * V, V), BF16),
            pltpu.VMEM((ITERS, ncol, 2 * V, V), BF16),
            pltpu.VMEM((ncol, 2 * V, V), BF16),
            pltpu.VMEM((ITERS, 2, V, V), BF16),
            pltpu.VMEM((ITERS, 2, V, V), BF16),
            pltpu.VMEM((2 * V, V), F32),
            pltpu.VMEM((2 * V, V), F32),
            pltpu.VMEM((2 * V, V), F32),
            pltpu.VMEM((2 * V, V), F32),
            pltpu.SMEM((2, ncol), F32),
            pltpu.SMEM((2, ncol), F32),
            pltpu.SMEM((2, 1, slots), jnp.int32),
            pltpu.SMEM((1, 2), jnp.int32),
            pltpu.SMEM((2, slots, ncol), jnp.int32),
            pltpu.SMEM((2, ncol), jnp.int32),
            pltpu.VMEM((1, V), F32),
            pltpu.SMEM((ncol,), F32),
            pltpu.SemaphoreType.DMA((ITERS, COUNT)),
            pltpu.SemaphoreType.DMA((ITERS, COUNT)),
            pltpu.SemaphoreType.DMA((10,)),
        ],
        compiler_params=pltpu.CompilerParams(
            collective_id=0, has_side_effects=True, vmem_limit_bytes=66000000
        ),
        name="sweeps",
    )(
        amplitudes,
        coulomb,
        inner_list,
        inner_count.T,
        reader_list.transpose(0, 2, 1),
        reader_count,
        virtual_energy.reshape(1, V),
        occupied_energy,
    )


def solution(mesh):
    return jax.shard_map(
        functools.partial(on_device, nrow=mesh.shape["row"], ncol=mesh.shape["col"]),
        mesh=mesh,
        in_specs=(
            P("row", "col", None, None),
            P("row", None, None, None),
            P("row", "col", None),
            P("row", "col"),
            P("row", None, None),
            P("row", None),
            P(),
            P(),
        ),
        out_specs=P("row", "col", None, None),
        check_vma=False,
    )
```

```python
import functools

import jax
import jax.numpy as jnp
from jax import lax
from jax.experimental import pallas as pl
from jax.experimental.pallas import tpu as pltpu
from jax.sharding import PartitionSpec as P

ITERS = 2

damping = 0.5
coupling = 0.03125
MESH = pl.DeviceIdType.MESH
F32 = jnp.float32
BF16 = jnp.bfloat16

Y_P, Y_Q, Y_QM, Y_QP, Y_Q2A, Y_Q2B = range(6)
R_Q, R_P, R_QA, R_NA, R_NB, R_PA, R_NRA = range(6, 13)
L_Q, L_P, L_QB, L_NB, L_NA, L_PB, L_NRB = range(13, 20)
COL = 20
N_P, N_Q = 40, 41
ZR_O, ZR_HP, ZR_HQ, ZR_OA, ZR_HA = range(42, 47)
ZL_O, ZL_HP, ZL_HQ, ZL_OB, ZL_HB = range(47, 52)
S_O, S_H, S_M, S_P, S_HM, S_HP, S_2, S_H2A, S_H2B = range(52, 61)
M_0, M_1, X_0, X_1 = range(61, 65)
COUNT = 65
LINEAR_CUT, COUPLED_CUT = 18, 14


def kernel(
    nrow, ncol, slots, V,
    amp_ref, coul_ref, ilist_ref, icnt_ref, rlist_ref, rcnt_ref, virt_ref, occ_ref,
    out_ref,
    amps, coups, rows, coul, mirror, transit, state, acc, base, inv, wlin, wquad,
    ilist, icnt, rlist, rcnt, virt, occ,
    send_sem, recv_sem, load_sem,
):
    r = lax.axis_index("row")
    c = lax.axis_index("col")

    def flip(v, bit):
        return v + bit - 2 * bit * lax.rem(v // bit, 2)

    unit = 2 * V // 32

    def cut(parts):
        first, rest = parts * unit, (32 - parts) * unit
        return dict(
            p=pl.ds(0, first), pa=pl.ds(0, first // 2), pb=pl.ds(first // 2, first // 2),
            q=pl.ds(first, rest), qa=pl.ds(first, rest // 2),
            qb=pl.ds(first + rest // 2, rest // 2),
        )

    lin, quad = cut(LINEAR_CUT), cut(COUPLED_CUT)
    cuts = {0: lin, COL: quad}
    half_a, half_b = pl.ds(0, V), pl.ds(V, V)

    ry = flip(r, 1)
    rp, rm, r2 = lax.rem(r + 2, nrow), lax.rem(r + nrow - 2, nrow), lax.rem(r + 4, nrow)
    yp, ym, y2 = flip(rp, 1), flip(rm, 1), flip(r2, 1)
    ch, cs = flip(c, 2), flip(c, 1)
    cp, cm, c2 = lax.rem(c + 4, ncol), lax.rem(c + ncol - 4, ncol), lax.rem(c + 8, ncol)
    hp, hm, h2 = flip(cp, 2), flip(cm, 2), flip(c2, 2)
    to_y, to_right, to_left = (ry, c), (rp, c), (rm, c)
    to_n, to_zr, to_zl, to_s = (ry, ch), (r, cp), (r, cm), (r, cs)
    to_zrs, to_zls = (r, flip(cp, 1)), (r, flip(cm, 1))
    nx = nrow // 2
    x, lo = r // 2, lax.rem(r, 2)
    z, hi, core = c // 4, lax.rem(c // 2, 2), lax.rem(c, 2)
    ahead = lax.rem(z - x + nx, nx)

    def place(px, pz, plo, phi, pcore):
        return (
            2 * lax.rem(px + nx, nx) + plo, 4 * lax.rem(pz + nx, nx) + 2 * phi + pcore
        )

    step = 2 - ahead
    diagonal = ahead == 0
    opposite = ahead == 2
    beside = jnp.logical_or(ahead == 1, ahead == 3)
    mself = tuple(
        jnp.logical_and(diagonal, jnp.logical_and(lo == hi, core == a)) for a in range(2)
    )
    mout = tuple(jnp.logical_and(diagonal, jnp.logical_not(mself[a])) for a in range(2))

    loads = [
        pltpu.make_async_copy(amp_ref.at[a, 0], state.at[pl.ds(a * V, V)], load_sem.at[a])
        for a in range(2)
    ]
    for a in range(2):
        loads[a].start()
    coul_loads = [
        pltpu.make_async_copy(
            coul_ref.at[a], coul.at[:, pl.ds(a * V, V)], load_sem.at[2 + a]
        )
        for a in range(2)
    ]
    for a in range(2):
        coul_loads[a].start()
    small_loads = [
        pltpu.make_async_copy(src, dst, load_sem.at[4 + at])
        for at, (src, dst) in enumerate((
            (ilist_ref, ilist), (icnt_ref, icnt), (rlist_ref, rlist), (rcnt_ref, rcnt),
            (virt_ref, virt), (occ_ref, occ),
        ))
    ]
    for load in small_loads:
        load.start()

    barrier = pltpu.get_barrier_semaphore()
    for dev in (to_y, to_right, to_left, to_n, to_zr, to_zl, to_s, to_zrs, to_zls):
        pl.semaphore_signal(barrier, inc=1, device_id=dev, device_id_type=MESH)

    def greet(condition, *devices):
        @pl.when(condition)
        def _():
            for dev in devices:
                pl.semaphore_signal(barrier, inc=1, device_id=dev, device_id_type=MESH)

    greet(diagonal, place(x, z + 1, hi, lo, core), place(x, z - 1, hi, lo, core))
    for a in range(2):
        greet(mout[a], place(x, z, hi, lo, a))
        greet(jnp.logical_and(beside, core == 0), place(z, x, hi, lo, a))
        greet(jnp.logical_and(beside, core == 1), place(z, z, lo, hi, a))
        greet(jnp.logical_and(opposite, core == 0), place(x - 1, z, lo, hi, a))
        greet(jnp.logical_and(opposite, core == 1), place(x + 1, z, lo, hi, a))
    greet(beside, place(x - step, z, lo, hi, core), place(x, z + 2, hi, lo, core))
    for condition, count in (
        (jnp.logical_or(beside, jnp.logical_and(diagonal, lo != hi)), 13),
        (jnp.logical_and(diagonal, lo == hi), 12),
        (opposite, 11),
    ):
        @pl.when(condition)
        def _():
            pl.semaphore_wait(barrier, count)

    for a in range(2):
        loads[a].wait()

    def sweep(s, carry):
        def message(src, dst, key, dev, recv_key=None):
            return pltpu.make_async_remote_copy(
                src_ref=src, dst_ref=dst, send_sem=send_sem.at[s, key],
                recv_sem=recv_sem.at[s, key if recv_key is None else recv_key],
                device_id=dev, device_id_type=MESH,
            )

        def send(ref, key, dev):
            message(ref, ref, key, dev).start()

        def arrived(ref, key):
            message(ref, ref, key, to_y).wait_recv()

        def consume(left, weight, right, source, first=False):
            for b in range(2):
                orbital = 2 * source + b
                block = right[s, source, b * V:(b + 1) * V, :]
                for a in range(2):
                    at = slice(a * V, (a + 1) * V)
                    part = jnp.dot(left(orbital, a), block, preferred_element_type=F32)
                    part = part * weight[a, orbital]
                    if first and b == 0:
                        acc[at, :] = part
                    else:
                        acc[at, :] += part

        def open_q(buf, o):
            k = cuts[o]
            own = buf.at[s, r]
            send(own.at[k["p"]], o + Y_P, to_y)
            send(own.at[k["q"]], o + R_Q, to_right)
            send(own.at[k["q"]], o + L_Q, to_left)
            send(own.at[k["q"]], o + Y_Q, to_y)

        def open_p(buf, o):
            k = cuts[o]
            own = buf.at[s, r]
            send(own.at[k["p"]], o + R_P, to_right)
            send(own.at[k["p"]], o + L_P, to_left)

        def relay_q(buf, o):
            k = cuts[o]
            arrived(buf.at[s, rm, k["q"]], o + R_Q)
            send(buf.at[s, rm, k["qa"]], o + R_QA, to_right)
            send(buf.at[s, rm, k["q"]], o + Y_QM, to_y)
            arrived(buf.at[s, rp, k["q"]], o + L_Q)
            send(buf.at[s, rp, k["qb"]], o + L_QB, to_left)
            send(buf.at[s, rp, k["q"]], o + Y_QP, to_y)

        def relay_n(buf, o):
            k = cuts[o]
            arrived(buf.at[s, ry, k["p"]], o + Y_P)
            send(buf.at[s, ry, k["pa"]], o + R_NA, to_right)
            send(buf.at[s, ry, k["pb"]], o + L_NB, to_left)
            send(buf.at[s, ry, k["pb"]], o + R_NB, to_right)
            send(buf.at[s, ry, k["pa"]], o + L_NA, to_left)

        def relay_p(buf, o):
            k = cuts[o]
            arrived(buf.at[s, rm, k["p"]], o + R_P)
            send(buf.at[s, rm, k["pa"]], o + R_PA, to_right)
            arrived(buf.at[s, rp, k["p"]], o + L_P)
            send(buf.at[s, rp, k["pb"]], o + L_PB, to_left)

        def relay_q2(buf, o):
            k = cuts[o]
            arrived(buf.at[s, r2, k["qa"]], o + R_QA)
            send(buf.at[s, r2, k["qa"]], o + Y_Q2A, to_y)
            arrived(buf.at[s, r2, k["qb"]], o + L_QB)
            send(buf.at[s, r2, k["qb"]], o + Y_Q2B, to_y)

        def relay_nn(buf, o):
            k = cuts[o]
            arrived(buf.at[s, ym, k["pa"]], o + R_NA)
            send(buf.at[s, ym, k["pa"]], o + R_NRA, to_right)
            arrived(buf.at[s, yp, k["pb"]], o + L_NB)
            send(buf.at[s, yp, k["pb"]], o + L_NRB, to_left)
            arrived(buf.at[s, ym, k["pb"]], o + R_NB)
            arrived(buf.at[s, yp, k["pa"]], o + L_NA)

        def lin_left(orbital, a):
            return coul[orbital, a * V:(a + 1) * V, :]

        def quad_left(orbital, a):
            return rows[s, orbital, a * V:(a + 1) * V, :]

        start = state[...].astype(BF16)
        amps[s, r] = start
        rows[s, c] = start
        open_q(amps, 0)
        open_p(amps, 0)
        send(rows.at[s, c], ZR_O, to_zr)
        send(rows.at[s, c], ZL_O, to_zl)
        send(rows.at[s, c], S_O, to_s)

        @pl.when(s == 0)
        def _():
            for load in small_loads:
                load.wait()
            for weight, entries, count in (
                (wlin, lambda a, t: ilist[a, 0, t], lambda a: icnt[0, a]),
                (wquad, lambda a, t: rlist[a, t, c], lambda a: rcnt[a, c]),
            ):
                for a in range(2):
                    used = count(a)
                    listed = [jnp.where(t < used, entries(a, t), -1) for t in range(slots)]
                    for orbital in range(ncol):
                        hit = listed[0] == orbital
                        for t in range(1, slots):
                            hit = jnp.logical_or(hit, listed[t] == orbital)
                        weight[a, orbital] = jnp.where(hit, 1.0, 0.0).astype(F32)
            across = jnp.broadcast_to(virt[...], (V, V))
            pair = across + across.T
            for a in range(2):
                inv[a * V:(a + 1) * V, :] = 1.0 / (pair - occ[2 * r + a] - occ[c])
            for a in range(2):
                coul_loads[a].wait()

        consume(lin_left, wlin, amps, r, first=True)
        relay_q(amps, 0)
        relay_n(amps, 0)
        message(amps.at[s, ry, lin["p"]], rows.at[s, c, lin["p"]], N_P, to_n).start()
        relay_p(amps, 0)
        arrived(amps.at[s, ry, lin["q"]], Y_Q)
        message(amps.at[s, ry, lin["q"]], rows.at[s, c, lin["q"]], N_Q, to_n).start()
        arrived(rows.at[s, cm], ZR_O)
        send(rows.at[s, cm, half_a], ZR_OA, to_zr)
        send(rows.at[s, cm], S_M, to_s)
        arrived(rows.at[s, cp], ZL_O)
        send(rows.at[s, cp, half_b], ZL_OB, to_zl)
        send(rows.at[s, cp], S_P, to_s)
        consume(lin_left, wlin, amps, rm)
        relay_q2(amps, 0)
        consume(lin_left, wlin, amps, rp)
        consume(lin_left, wlin, amps, ry)
        arrived(rows.at[s, ch, lin["p"]], N_P)
        send(rows.at[s, ch, lin["p"]], ZR_HP, to_zr)
        send(rows.at[s, ch, lin["p"]], ZL_HP, to_zl)
        relay_nn(amps, 0)
        arrived(rows.at[s, ch, lin["q"]], N_Q)
        send(rows.at[s, ch, lin["q"]], ZR_HQ, to_zr)
        send(rows.at[s, ch, lin["q"]], ZL_HQ, to_zl)
        send(rows.at[s, ch], S_H, to_s)
        arrived(amps.at[s, ym, lin["q"]], Y_QM)
        consume(lin_left, wlin, amps, ym)
        arrived(amps.at[s, yp, lin["q"]], Y_QP)
        consume(lin_left, wlin, amps, yp)
        arrived(amps.at[s, r2, lin["pa"]], R_PA)
        arrived(amps.at[s, r2, lin["pb"]], L_PB)
        consume(lin_left, wlin, amps, r2)
        arrived(rows.at[s, c2, half_a], ZR_OA)
        arrived(rows.at[s, c2, half_b], ZL_OB)
        send(rows.at[s, c2], S_2, to_s)
        arrived(amps.at[s, y2, lin["qa"]], Y_Q2A)
        arrived(amps.at[s, y2, lin["qb"]], Y_Q2B)
        arrived(amps.at[s, y2, lin["pa"]], R_NRA)
        arrived(amps.at[s, y2, lin["pb"]], L_NRB)
        consume(lin_left, wlin, amps, y2)

        coups[s, r] = acc[...].astype(BF16)
        block = [coups.at[s, r, half_a], coups.at[s, r, half_b]]
        final = (mirror.at[s, core], M_0 + core)

        def forward(src, key, target, dev):
            message(src, target[0], key, dev, target[1]).start()

        open_q(coups, COL)

        @pl.when(opposite)
        def _():
            first = (transit.at[s, 0], X_0)
            forward(block[0], M_0, first, place(x + 1, z, lo, hi, core))
            forward(block[1], M_1, first, place(x - 1, z, lo, hi, core))

        open_p(coups, COL)

        @pl.when(beside)
        def _():
            crossing = ahead // 2
            forward(
                block[1], M_1, (transit.at[s, crossing], X_0 + crossing),
                place(x, x, hi, lo, core),
            )
            forward(block[0], M_0, final, place(z, x, hi, lo, 0))

        for a in range(2):
            @pl.when(mout[a])
            def _():
                forward(block[a], M_0 + a, final, place(x, z, hi, lo, a))

            @pl.when(mself[a])
            def _():
                mirror[s, a] = coups[s, r, a * V:(a + 1) * V, :]

        for a in range(2):
            at = slice(a * V, (a + 1) * V)
            linear = coul[c, at, :].astype(F32) + coupling * coups[s, r, at, :].astype(F32)
            base[at, :] = damping * state[at, :] - linear * inv[at, :]
        arrived(rows.at[s, hm, lin["p"]], ZR_HP)
        send(rows.at[s, hm, half_a], ZR_HA, to_zr)
        send(rows.at[s, hm, half_a], S_H2A, to_zrs)
        arrived(rows.at[s, hp, lin["p"]], ZL_HP)
        arrived(rows.at[s, hp, lin["q"]], ZL_HQ)
        send(rows.at[s, hp, half_b], ZL_HB, to_zl)
        send(rows.at[s, hp, half_b], S_H2B, to_zls)
        arrived(rows.at[s, hm, lin["q"]], ZR_HQ)
        send(rows.at[s, hm], S_HM, to_s)
        send(rows.at[s, hp], S_HP, to_s)
        relay_q(coups, COL)
        relay_n(coups, COL)

        @pl.when(diagonal)
        def _():
            for at, px in ((0, x + 1), (1, x - 1)):
                arrived(transit.at[s, at], X_0 + at)
                forward(transit.at[s, at], X_0 + at, final, place(px, z, lo, hi, 1))

        @pl.when(beside)
        def _():
            arrived(transit.at[s, 0], X_0)
            forward(
                transit.at[s, 0], X_0, (transit.at[s, 1], X_1), place(x, z + 2, hi, lo, core)
            )

        relay_p(coups, COL)
        relay_q2(coups, COL)
        arrived(coups.at[s, ry, quad["q"]], COL + Y_Q)
        for own, key in (
            (c, S_O), (ch, S_H), (cm, S_M), (cp, S_P), (hm, S_HM), (hp, S_HP), (c2, S_2),
        ):
            arrived(rows.at[s, flip(own, 1)], key)
        arrived(rows.at[s, h2, half_a], ZR_HA)
        arrived(rows.at[s, h2, half_b], ZL_HB)
        arrived(rows.at[s, flip(h2, 1), half_a], S_H2A)
        arrived(rows.at[s, flip(h2, 1), half_b], S_H2B)
        consume(quad_left, wquad, coups, r, first=True)
        consume(quad_left, wquad, coups, rm)
        relay_nn(coups, COL)

        @pl.when(beside)
        def _():
            arrived(transit.at[s, 1], X_1)
            forward(transit.at[s, 1], X_1, final, place(x - step, z, lo, hi, ahead % 3))

        consume(quad_left, wquad, coups, rp)
        consume(quad_left, wquad, coups, ry)
        arrived(coups.at[s, ym, quad["q"]], COL + Y_QM)
        consume(quad_left, wquad, coups, ym)
        arrived(coups.at[s, yp, quad["q"]], COL + Y_QP)
        consume(quad_left, wquad, coups, yp)
        arrived(coups.at[s, r2, quad["pa"]], COL + R_PA)
        arrived(coups.at[s, r2, quad["pb"]], COL + L_PB)
        consume(quad_left, wquad, coups, r2)
        for a in range(2):
            @pl.when(jnp.logical_not(mself[a]))
            def _():
                arrived(mirror.at[s, a], M_0 + a)

            at = slice(a * V, (a + 1) * V)
            flipped = mirror[s, a].astype(F32).T
            base[at, :] -= coupling * flipped * inv[at, :]
        arrived(coups.at[s, y2, quad["qa"]], COL + Y_Q2A)
        arrived(coups.at[s, y2, quad["qb"]], COL + Y_Q2B)
        arrived(coups.at[s, y2, quad["pa"]], COL + R_NRA)
        arrived(coups.at[s, y2, quad["pb"]], COL + L_NRB)
        consume(quad_left, wquad, coups, y2)
        state[...] = base[...] - (coupling * coupling) * acc[...] * inv[...]
        return carry

    lax.fori_loop(0, ITERS, sweep, 0)
    for a in range(2):
        out_ref[a, 0] = state[a * V:(a + 1) * V, :]
    sizes = {}
    for o, k in cuts.items():
        for keys, part in (
            ((Y_P, R_P, L_P), "p"),
            ((Y_Q, Y_QM, Y_QP, R_Q, L_Q), "q"),
            ((Y_Q2A, Y_Q2B, R_QA, L_QB), "qa"),
            ((R_NA, R_NB, R_PA, R_NRA, L_NB, L_NA, L_PB, L_NRB), "pa"),
        ):
            for key in keys:
                sizes[o + key] = amps.at[0, r, k[part]]
    sizes[N_P], sizes[N_Q] = amps.at[0, r, lin["p"]], amps.at[0, r, lin["q"]]
    for part, keys in (("p", (ZR_HP, ZL_HP)), ("q", (ZR_HQ, ZL_HQ))):
        for key in keys:
            sizes[key] = rows.at[0, c, lin[part]]
    for key in (ZR_O, ZL_O, *range(S_O, S_H2A)):
        sizes[key] = rows.at[0, c]
    for key in (ZR_OA, ZR_HA, ZL_OB, ZL_HB, S_H2A, S_H2B):
        sizes[key] = rows.at[0, c, half_a]

    def drain(s, carry):
        def sent(ref, key):
            pltpu.make_async_remote_copy(
                src_ref=ref, dst_ref=ref, send_sem=send_sem.at[s, key],
                recv_sem=recv_sem.at[s, key], device_id=to_y, device_id_type=MESH,
            ).wait_send()

        for key, ref in sizes.items():
            sent(ref, key)
        for a in range(2):
            @pl.when(jnp.logical_not(mself[a]))
            def _():
                sent(mirror.at[0, a], M_0 + a)

        @pl.when(jnp.logical_not(opposite))
        def _():
            for a in range(2):
                sent(transit.at[0, a], X_0 + a)

        return carry

    lax.fori_loop(0, ITERS, drain, 0)


def on_device(
    amplitudes,
    coulomb,
    inner_list,
    inner_count,
    reader_list,
    reader_count,
    virtual_energy,
    occupied_energy,
    *,
    nrow,
    ncol,
):
    V = amplitudes.shape[2]
    slots = inner_list.shape[2]
    hbm = pl.BlockSpec(memory_space=pltpu.HBM)
    vmem = pl.BlockSpec(memory_space=pltpu.VMEM)
    return pl.pallas_call(
        functools.partial(kernel, nrow, ncol, slots, V),
        out_shape=pltpu.VMEM(amplitudes.shape, F32),
        in_specs=[hbm] * 8,
        out_specs=vmem,
        scratch_shapes=[
            pltpu.VMEM((ITERS, nrow, 2 * V, V), BF16),
            pltpu.VMEM((ITERS, nrow, 2 * V, V), BF16),
            pltpu.VMEM((ITERS, ncol, 2 * V, V), BF16),
            pltpu.VMEM((ncol, 2 * V, V), BF16),
            pltpu.VMEM((ITERS, 2, V, V), BF16),
            pltpu.VMEM((ITERS, 2, V, V), BF16),
            pltpu.VMEM((2 * V, V), F32),
            pltpu.VMEM((2 * V, V), F32),
            pltpu.VMEM((2 * V, V), F32),
            pltpu.VMEM((2 * V, V), F32),
            pltpu.SMEM((2, ncol), F32),
            pltpu.SMEM((2, ncol), F32),
            pltpu.SMEM((2, 1, slots), jnp.int32),
            pltpu.SMEM((1, 2), jnp.int32),
            pltpu.SMEM((2, slots, ncol), jnp.int32),
            pltpu.SMEM((2, ncol), jnp.int32),
            pltpu.VMEM((1, V), F32),
            pltpu.SMEM((ncol,), F32),
            pltpu.SemaphoreType.DMA((ITERS, COUNT)),
            pltpu.SemaphoreType.DMA((ITERS, COUNT)),
            pltpu.SemaphoreType.DMA((10,)),
        ],
        compiler_params=pltpu.CompilerParams(
            collective_id=0, has_side_effects=True, vmem_limit_bytes=66000000
        ),
        name="sweeps",
    )(
        amplitudes,
        coulomb,
        inner_list,
        inner_count.T,
        reader_list.transpose(0, 2, 1),
        reader_count,
        virtual_energy.reshape(1, V),
        occupied_energy,
    )


def solution(mesh):
    return jax.shard_map(
        functools.partial(on_device, nrow=mesh.shape["row"], ncol=mesh.shape["col"]),
        mesh=mesh,
        in_specs=(
            P("row", "col", None, None),
            P("row", None, None, None),
            P("row", "col", None),
            P("row", "col"),
            P("row", None, None),
            P("row", None),
            P(),
            P(),
        ),
        out_specs=P("row", "col", None, None),
        check_vma=False,
    )
```

```python
import functools

import jax
import jax.numpy as jnp
from jax import lax
from jax.experimental import pallas as pl
from jax.experimental.pallas import tpu as pltpu
from jax.sharding import PartitionSpec as P

ITERS = 2

damping = 0.5
coupling = 0.03125
MESH = pl.DeviceIdType.MESH
F32 = jnp.float32
BF16 = jnp.bfloat16

Y_P, Y_Q, Y_QM, Y_QP, Y_Q2A, Y_Q2B = range(6)
R_Q, R_P, R_QA, R_NA, R_NB, R_PA, R_NRA = range(6, 13)
L_Q, L_P, L_QB, L_NB, L_NA, L_PB, L_NRB = range(13, 20)
COL = 20
N_P, N_Q = 40, 41
ZR_O, ZR_HP, ZR_HQ, ZR_OA, ZR_HA = range(42, 47)
ZL_O, ZL_HP, ZL_HQ, ZL_OB, ZL_HB = range(47, 52)
S_O, S_H, S_M, S_P, S_HM, S_HP, S_2, S_H2A, S_H2B = range(52, 61)
M_0, M_1, X_0, X_1 = range(61, 65)
COUNT = 65
LINEAR_CUT, COUPLED_CUT = 18, 14


def kernel(
    nrow, ncol, slots, V,
    amp_ref, coul_ref, ilist_ref, icnt_ref, rlist_ref, rcnt_ref, virt_ref, occ_ref,
    out_ref,
    amps, coups, rows, coul, mirror, transit, state, acc, base, inv, wlin, wquad,
    ilist, icnt, rlist, rcnt, virt, occ,
    send_sem, recv_sem, load_sem,
):
    r = lax.axis_index("row")
    c = lax.axis_index("col")

    def flip(v, bit):
        return v + bit - 2 * bit * lax.rem(v // bit, 2)

    unit = 2 * V // 32

    def cut(parts):
        first, rest = parts * unit, (32 - parts) * unit
        return dict(
            p=pl.ds(0, first), pa=pl.ds(0, first // 2), pb=pl.ds(first // 2, first // 2),
            q=pl.ds(first, rest), qa=pl.ds(first, rest // 2),
            qb=pl.ds(first + rest // 2, rest // 2),
        )

    lin, quad = cut(LINEAR_CUT), cut(COUPLED_CUT)
    cuts = {0: lin, COL: quad}
    half_a, half_b = pl.ds(0, V), pl.ds(V, V)

    ry = flip(r, 1)
    rp, rm, r2 = lax.rem(r + 2, nrow), lax.rem(r + nrow - 2, nrow), lax.rem(r + 4, nrow)
    yp, ym, y2 = flip(rp, 1), flip(rm, 1), flip(r2, 1)
    ch, cs = flip(c, 2), flip(c, 1)
    cp, cm, c2 = lax.rem(c + 4, ncol), lax.rem(c + ncol - 4, ncol), lax.rem(c + 8, ncol)
    hp, hm, h2 = flip(cp, 2), flip(cm, 2), flip(c2, 2)
    to_y, to_right, to_left = (ry, c), (rp, c), (rm, c)
    to_n, to_zr, to_zl, to_s = (ry, ch), (r, cp), (r, cm), (r, cs)
    to_zrs, to_zls = (r, flip(cp, 1)), (r, flip(cm, 1))
    nx = nrow // 2
    x, lo = r // 2, lax.rem(r, 2)
    z, hi, core = c // 4, lax.rem(c // 2, 2), lax.rem(c, 2)
    ahead = lax.rem(z - x + nx, nx)

    def place(px, pz, plo, phi, pcore):
        return (
            2 * lax.rem(px + nx, nx) + plo, 4 * lax.rem(pz + nx, nx) + 2 * phi + pcore
        )

    step = 2 - ahead
    diagonal = ahead == 0
    opposite = ahead == 2
    beside = jnp.logical_or(ahead == 1, ahead == 3)
    mself = tuple(
        jnp.logical_and(diagonal, jnp.logical_and(lo == hi, core == a)) for a in range(2)
    )
    mout = tuple(jnp.logical_and(diagonal, jnp.logical_not(mself[a])) for a in range(2))

    loads = [
        pltpu.make_async_copy(amp_ref.at[a, 0], state.at[pl.ds(a * V, V)], load_sem.at[a])
        for a in range(2)
    ]
    for a in range(2):
        loads[a].start()
    coul_loads = [
        pltpu.make_async_copy(
            coul_ref.at[a], coul.at[:, pl.ds(a * V, V)], load_sem.at[2 + a]
        )
        for a in range(2)
    ]
    for a in range(2):
        coul_loads[a].start()
    small_loads = [
        pltpu.make_async_copy(src, dst, load_sem.at[4 + at])
        for at, (src, dst) in enumerate((
            (ilist_ref, ilist), (icnt_ref, icnt), (rlist_ref, rlist), (rcnt_ref, rcnt),
            (virt_ref, virt), (occ_ref, occ),
        ))
    ]
    for load in small_loads:
        load.start()

    barrier = pltpu.get_barrier_semaphore()
    for dev in (to_y, to_right, to_left, to_n, to_zr, to_zl, to_s, to_zrs, to_zls):
        pl.semaphore_signal(barrier, inc=1, device_id=dev, device_id_type=MESH)

    def greet(condition, *devices):
        @pl.when(condition)
        def _():
            for dev in devices:
                pl.semaphore_signal(barrier, inc=1, device_id=dev, device_id_type=MESH)

    greet(diagonal, place(x, z + 1, hi, lo, core), place(x, z - 1, hi, lo, core))
    for a in range(2):
        greet(mout[a], place(x, z, hi, lo, a))
        greet(jnp.logical_and(beside, core == 0), place(z, x, hi, lo, a))
        greet(jnp.logical_and(beside, core == 1), place(z, z, lo, hi, a))
        greet(jnp.logical_and(opposite, core == 0), place(x - 1, z, lo, hi, a))
        greet(jnp.logical_and(opposite, core == 1), place(x + 1, z, lo, hi, a))
    greet(beside, place(x - step, z, lo, hi, core), place(x, z + 2, hi, lo, core))
    for condition, count in (
        (jnp.logical_or(beside, jnp.logical_and(diagonal, lo != hi)), 13),
        (jnp.logical_and(diagonal, lo == hi), 12),
        (opposite, 11),
    ):
        @pl.when(condition)
        def _():
            pl.semaphore_wait(barrier, count)

    for a in range(2):
        loads[a].wait()

    def sweep(s, carry):
        def message(src, dst, key, dev, recv_key=None):
            return pltpu.make_async_remote_copy(
                src_ref=src, dst_ref=dst, send_sem=send_sem.at[s, key],
                recv_sem=recv_sem.at[s, key if recv_key is None else recv_key],
                device_id=dev, device_id_type=MESH,
            )

        def send(ref, key, dev):
            message(ref, ref, key, dev).start()

        def arrived(ref, key):
            message(ref, ref, key, to_y).wait_recv()

        def consume(left, weight, right, source, first=False):
            for b in range(2):
                orbital = 2 * source + b
                block = right[s, source, b * V:(b + 1) * V, :]
                for a in range(2):
                    at = slice(a * V, (a + 1) * V)
                    part = jnp.dot(left(orbital, a), block, preferred_element_type=F32)
                    part = part * weight[a, orbital]
                    if first and b == 0:
                        acc[at, :] = part
                    else:
                        acc[at, :] += part

        def open_q(buf, o):
            k = cuts[o]
            own = buf.at[s, r]
            send(own.at[k["p"]], o + Y_P, to_y)
            send(own.at[k["q"]], o + R_Q, to_right)
            send(own.at[k["q"]], o + L_Q, to_left)
            send(own.at[k["q"]], o + Y_Q, to_y)

        def open_p(buf, o):
            k = cuts[o]
            own = buf.at[s, r]
            send(own.at[k["p"]], o + R_P, to_right)
            send(own.at[k["p"]], o + L_P, to_left)

        def relay_q(buf, o):
            k = cuts[o]
            arrived(buf.at[s, rm, k["q"]], o + R_Q)
            send(buf.at[s, rm, k["qa"]], o + R_QA, to_right)
            send(buf.at[s, rm, k["q"]], o + Y_QM, to_y)
            arrived(buf.at[s, rp, k["q"]], o + L_Q)
            send(buf.at[s, rp, k["qb"]], o + L_QB, to_left)
            send(buf.at[s, rp, k["q"]], o + Y_QP, to_y)

        def relay_n(buf, o):
            k = cuts[o]
            arrived(buf.at[s, ry, k["p"]], o + Y_P)
            send(buf.at[s, ry, k["pa"]], o + R_NA, to_right)
            send(buf.at[s, ry, k["pb"]], o + L_NB, to_left)
            send(buf.at[s, ry, k["pb"]], o + R_NB, to_right)
            send(buf.at[s, ry, k["pa"]], o + L_NA, to_left)

        def relay_p(buf, o):
            k = cuts[o]
            arrived(buf.at[s, rm, k["p"]], o + R_P)
            send(buf.at[s, rm, k["pa"]], o + R_PA, to_right)
            arrived(buf.at[s, rp, k["p"]], o + L_P)
            send(buf.at[s, rp, k["pb"]], o + L_PB, to_left)

        def relay_q2(buf, o):
            k = cuts[o]
            arrived(buf.at[s, r2, k["qa"]], o + R_QA)
            send(buf.at[s, r2, k["qa"]], o + Y_Q2A, to_y)
            arrived(buf.at[s, r2, k["qb"]], o + L_QB)
            send(buf.at[s, r2, k["qb"]], o + Y_Q2B, to_y)

        def relay_nn(buf, o):
            k = cuts[o]
            arrived(buf.at[s, ym, k["pa"]], o + R_NA)
            send(buf.at[s, ym, k["pa"]], o + R_NRA, to_right)
            arrived(buf.at[s, yp, k["pb"]], o + L_NB)
            send(buf.at[s, yp, k["pb"]], o + L_NRB, to_left)
            arrived(buf.at[s, ym, k["pb"]], o + R_NB)
            arrived(buf.at[s, yp, k["pa"]], o + L_NA)

        def lin_left(orbital, a):
            return coul[orbital, a * V:(a + 1) * V, :]

        def quad_left(orbital, a):
            return rows[s, orbital, a * V:(a + 1) * V, :]

        start = state[...].astype(BF16)
        amps[s, r] = start
        rows[s, c] = start
        open_q(amps, 0)
        open_p(amps, 0)
        send(rows.at[s, c], ZR_O, to_zr)
        send(rows.at[s, c], ZL_O, to_zl)
        send(rows.at[s, c], S_O, to_s)

        @pl.when(s == 0)
        def _():
            for load in small_loads:
                load.wait()
            for weight, entries, count in (
                (wlin, lambda a, t: ilist[a, 0, t], lambda a: icnt[0, a]),
                (wquad, lambda a, t: rlist[a, t, c], lambda a: rcnt[a, c]),
            ):
                for a in range(2):
                    used = count(a)
                    listed = [jnp.where(t < used, entries(a, t), -1) for t in range(slots)]
                    for orbital in range(ncol):
                        hit = listed[0] == orbital
                        for t in range(1, slots):
                            hit = jnp.logical_or(hit, listed[t] == orbital)
                        weight[a, orbital] = jnp.where(hit, 1.0, 0.0).astype(F32)
            across = jnp.broadcast_to(virt[...], (V, V))
            pair = across + across.T
            for a in range(2):
                inv[a * V:(a + 1) * V, :] = 1.0 / (pair - occ[2 * r + a] - occ[c])
            for a in range(2):
                coul_loads[a].wait()

        consume(lin_left, wlin, amps, r, first=True)
        relay_q(amps, 0)
        relay_n(amps, 0)
        message(amps.at[s, ry, lin["p"]], rows.at[s, c, lin["p"]], N_P, to_n).start()
        relay_p(amps, 0)
        arrived(amps.at[s, ry, lin["q"]], Y_Q)
        message(amps.at[s, ry, lin["q"]], rows.at[s, c, lin["q"]], N_Q, to_n).start()
        arrived(rows.at[s, cm], ZR_O)
        send(rows.at[s, cm, half_a], ZR_OA, to_zr)
        send(rows.at[s, cm], S_M, to_s)
        arrived(rows.at[s, cp], ZL_O)
        send(rows.at[s, cp, half_b], ZL_OB, to_zl)
        send(rows.at[s, cp], S_P, to_s)
        consume(lin_left, wlin, amps, rm)
        relay_q2(amps, 0)
        consume(lin_left, wlin, amps, rp)
        consume(lin_left, wlin, amps, ry)
        arrived(rows.at[s, ch, lin["p"]], N_P)
        send(rows.at[s, ch, lin["p"]], ZR_HP, to_zr)
        send(rows.at[s, ch, lin["p"]], ZL_HP, to_zl)
        relay_nn(amps, 0)
        arrived(rows.at[s, ch, lin["q"]], N_Q)
        send(rows.at[s, ch, lin["q"]], ZR_HQ, to_zr)
        send(rows.at[s, ch, lin["q"]], ZL_HQ, to_zl)
        send(rows.at[s, ch], S_H, to_s)
        arrived(amps.at[s, ym, lin["q"]], Y_QM)
        consume(lin_left, wlin, amps, ym)
        arrived(amps.at[s, yp, lin["q"]], Y_QP)
        consume(lin_left, wlin, amps, yp)
        arrived(amps.at[s, r2, lin["pa"]], R_PA)
        arrived(amps.at[s, r2, lin["pb"]], L_PB)
        consume(lin_left, wlin, amps, r2)
        arrived(rows.at[s, c2, half_a], ZR_OA)
        arrived(rows.at[s, c2, half_b], ZL_OB)
        send(rows.at[s, c2], S_2, to_s)
        arrived(amps.at[s, y2, lin["qa"]], Y_Q2A)
        arrived(amps.at[s, y2, lin["qb"]], Y_Q2B)
        arrived(amps.at[s, y2, lin["pa"]], R_NRA)
        arrived(amps.at[s, y2, lin["pb"]], L_NRB)
        consume(lin_left, wlin, amps, y2)

        coups[s, r] = acc[...].astype(BF16)
        block = [coups.at[s, r, half_a], coups.at[s, r, half_b]]
        final = (mirror.at[s, core], M_0 + core)

        def forward(src, key, target, dev):
            message(src, target[0], key, dev, target[1]).start()

        open_q(coups, COL)

        @pl.when(opposite)
        def _():
            first = (transit.at[s, 0], X_0)
            forward(block[0], M_0, first, place(x + 1, z, lo, hi, core))
            forward(block[1], M_1, first, place(x - 1, z, lo, hi, core))

        open_p(coups, COL)

        @pl.when(beside)
        def _():
            crossing = ahead // 2
            forward(
                block[1], M_1, (transit.at[s, crossing], X_0 + crossing),
                place(x, x, hi, lo, core),
            )
            forward(block[0], M_0, final, place(z, x, hi, lo, 0))

        for a in range(2):
            @pl.when(mout[a])
            def _():
                forward(block[a], M_0 + a, final, place(x, z, hi, lo, a))

            @pl.when(mself[a])
            def _():
                mirror[s, a] = coups[s, r, a * V:(a + 1) * V, :]

        for a in range(2):
            at = slice(a * V, (a + 1) * V)
            linear = coul[c, at, :].astype(F32) + coupling * coups[s, r, at, :].astype(F32)
            base[at, :] = damping * state[at, :] - linear * inv[at, :]
        arrived(rows.at[s, hm, lin["p"]], ZR_HP)
        send(rows.at[s, hm, half_a], ZR_HA, to_zr)
        send(rows.at[s, hm, half_a], S_H2A, to_zrs)
        arrived(rows.at[s, hp, lin["p"]], ZL_HP)
        arrived(rows.at[s, hp, lin["q"]], ZL_HQ)
        send(rows.at[s, hp, half_b], ZL_HB, to_zl)
        send(rows.at[s, hp, half_b], S_H2B, to_zls)
        arrived(rows.at[s, hm, lin["q"]], ZR_HQ)
        send(rows.at[s, hm], S_HM, to_s)
        send(rows.at[s, hp], S_HP, to_s)
        relay_q(coups, COL)
        relay_n(coups, COL)

        @pl.when(diagonal)
        def _():
            for at, px in ((0, x + 1), (1, x - 1)):
                arrived(transit.at[s, at], X_0 + at)
                forward(transit.at[s, at], X_0 + at, final, place(px, z, lo, hi, 1))

        @pl.when(beside)
        def _():
            arrived(transit.at[s, 0], X_0)
            forward(
                transit.at[s, 0], X_0, (transit.at[s, 1], X_1), place(x, z + 2, hi, lo, core)
            )

        relay_p(coups, COL)
        relay_q2(coups, COL)

        @pl.when(beside)
        def _():
            arrived(transit.at[s, 1], X_1)
            forward(transit.at[s, 1], X_1, final, place(x - step, z, lo, hi, ahead % 3))

        relay_nn(coups, COL)
        arrived(coups.at[s, ry, quad["q"]], COL + Y_Q)
        for own, key in (
            (c, S_O), (ch, S_H), (cm, S_M), (cp, S_P), (hm, S_HM), (hp, S_HP), (c2, S_2),
        ):
            arrived(rows.at[s, flip(own, 1)], key)
        arrived(rows.at[s, h2, half_a], ZR_HA)
        arrived(rows.at[s, h2, half_b], ZL_HB)
        arrived(rows.at[s, flip(h2, 1), half_a], S_H2A)
        arrived(rows.at[s, flip(h2, 1), half_b], S_H2B)
        consume(quad_left, wquad, coups, r, first=True)
        consume(quad_left, wquad, coups, rm)

        consume(quad_left, wquad, coups, rp)
        consume(quad_left, wquad, coups, ry)
        arrived(coups.at[s, ym, quad["q"]], COL + Y_QM)
        consume(quad_left, wquad, coups, ym)
        arrived(coups.at[s, yp, quad["q"]], COL + Y_QP)
        consume(quad_left, wquad, coups, yp)
        arrived(coups.at[s, r2, quad["pa"]], COL + R_PA)
        arrived(coups.at[s, r2, quad["pb"]], COL + L_PB)
        consume(quad_left, wquad, coups, r2)
        for a in range(2):
            @pl.when(jnp.logical_not(mself[a]))
            def _():
                arrived(mirror.at[s, a], M_0 + a)

            at = slice(a * V, (a + 1) * V)
            flipped = mirror[s, a].astype(F32).T
            base[at, :] -= coupling * flipped * inv[at, :]
        arrived(coups.at[s, y2, quad["qa"]], COL + Y_Q2A)
        arrived(coups.at[s, y2, quad["qb"]], COL + Y_Q2B)
        arrived(coups.at[s, y2, quad["pa"]], COL + R_NRA)
        arrived(coups.at[s, y2, quad["pb"]], COL + L_NRB)
        consume(quad_left, wquad, coups, y2)
        state[...] = base[...] - (coupling * coupling) * acc[...] * inv[...]
        return carry

    lax.fori_loop(0, ITERS, sweep, 0)
    for a in range(2):
        out_ref[a, 0] = state[a * V:(a + 1) * V, :]
    sizes = {}
    for o, k in cuts.items():
        for keys, part in (
            ((Y_P, R_P, L_P), "p"),
            ((Y_Q, Y_QM, Y_QP, R_Q, L_Q), "q"),
            ((Y_Q2A, Y_Q2B, R_QA, L_QB), "qa"),
            ((R_NA, R_NB, R_PA, R_NRA, L_NB, L_NA, L_PB, L_NRB), "pa"),
        ):
            for key in keys:
                sizes[o + key] = amps.at[0, r, k[part]]
    sizes[N_P], sizes[N_Q] = amps.at[0, r, lin["p"]], amps.at[0, r, lin["q"]]
    for part, keys in (("p", (ZR_HP, ZL_HP)), ("q", (ZR_HQ, ZL_HQ))):
        for key in keys:
            sizes[key] = rows.at[0, c, lin[part]]
    for key in (ZR_O, ZL_O, *range(S_O, S_H2A)):
        sizes[key] = rows.at[0, c]
    for key in (ZR_OA, ZR_HA, ZL_OB, ZL_HB, S_H2A, S_H2B):
        sizes[key] = rows.at[0, c, half_a]

    def drain(s, carry):
        def sent(ref, key):
            pltpu.make_async_remote_copy(
                src_ref=ref, dst_ref=ref, send_sem=send_sem.at[s, key],
                recv_sem=recv_sem.at[s, key], device_id=to_y, device_id_type=MESH,
            ).wait_send()

        for key, ref in sizes.items():
            sent(ref, key)
        for a in range(2):
            @pl.when(jnp.logical_not(mself[a]))
            def _():
                sent(mirror.at[0, a], M_0 + a)

        @pl.when(jnp.logical_not(opposite))
        def _():
            for a in range(2):
                sent(transit.at[0, a], X_0 + a)

        return carry

    lax.fori_loop(0, ITERS, drain, 0)


def on_device(
    amplitudes,
    coulomb,
    inner_list,
    inner_count,
    reader_list,
    reader_count,
    virtual_energy,
    occupied_energy,
    *,
    nrow,
    ncol,
):
    V = amplitudes.shape[2]
    slots = inner_list.shape[2]
    hbm = pl.BlockSpec(memory_space=pltpu.HBM)
    vmem = pl.BlockSpec(memory_space=pltpu.VMEM)
    return pl.pallas_call(
        functools.partial(kernel, nrow, ncol, slots, V),
        out_shape=pltpu.VMEM(amplitudes.shape, F32),
        in_specs=[hbm] * 8,
        out_specs=vmem,
        scratch_shapes=[
            pltpu.VMEM((ITERS, nrow, 2 * V, V), BF16),
            pltpu.VMEM((ITERS, nrow, 2 * V, V), BF16),
            pltpu.VMEM((ITERS, ncol, 2 * V, V), BF16),
            pltpu.VMEM((ncol, 2 * V, V), BF16),
            pltpu.VMEM((ITERS, 2, V, V), BF16),
            pltpu.VMEM((ITERS, 2, V, V), BF16),
            pltpu.VMEM((2 * V, V), F32),
            pltpu.VMEM((2 * V, V), F32),
            pltpu.VMEM((2 * V, V), F32),
            pltpu.VMEM((2 * V, V), F32),
            pltpu.SMEM((2, ncol), F32),
            pltpu.SMEM((2, ncol), F32),
            pltpu.SMEM((2, 1, slots), jnp.int32),
            pltpu.SMEM((1, 2), jnp.int32),
            pltpu.SMEM((2, slots, ncol), jnp.int32),
            pltpu.SMEM((2, ncol), jnp.int32),
            pltpu.VMEM((1, V), F32),
            pltpu.SMEM((ncol,), F32),
            pltpu.SemaphoreType.DMA((ITERS, COUNT)),
            pltpu.SemaphoreType.DMA((ITERS, COUNT)),
            pltpu.SemaphoreType.DMA((10,)),
        ],
        compiler_params=pltpu.CompilerParams(
            collective_id=0, has_side_effects=True, vmem_limit_bytes=66000000
        ),
        name="sweeps",
    )(
        amplitudes,
        coulomb,
        inner_list,
        inner_count.T,
        reader_list.transpose(0, 2, 1),
        reader_count,
        virtual_energy.reshape(1, V),
        occupied_energy,
    )


def solution(mesh):
    return jax.shard_map(
        functools.partial(on_device, nrow=mesh.shape["row"], ncol=mesh.shape["col"]),
        mesh=mesh,
        in_specs=(
            P("row", "col", None, None),
            P("row", None, None, None),
            P("row", "col", None),
            P("row", "col"),
            P("row", None, None),
            P("row", None),
            P(),
            P(),
        ),
        out_specs=P("row", "col", None, None),
        check_vma=False,
    )
```

```python
import functools

import jax
import jax.numpy as jnp
from jax import lax
from jax.experimental import pallas as pl
from jax.experimental.pallas import tpu as pltpu
from jax.sharding import PartitionSpec as P

ITERS = 2

damping = 0.5
coupling = 0.03125
MESH = pl.DeviceIdType.MESH
F32 = jnp.float32
BF16 = jnp.bfloat16

Y_P, Y_Q, Y_QM, Y_QP, Y_Q2A, Y_Q2B = range(6)
R_Q, R_P, R_QA, R_NA, R_NB, R_PA, R_NRA = range(6, 13)
L_Q, L_P, L_QB, L_NB, L_NA, L_PB, L_NRB = range(13, 20)
COL = 20
N_P, N_Q = 40, 41
ZR_O, ZR_HP, ZR_HQ, ZR_OA, ZR_HA = range(42, 47)
ZL_O, ZL_HP, ZL_HQ, ZL_OB, ZL_HB = range(47, 52)
S_O, S_H, S_M, S_P, S_HM, S_HP, S_2, S_H2A, S_H2B = range(52, 61)
M_0, M_1, X_0, X_1 = range(61, 65)
COUNT = 65
LINEAR_CUT, COUPLED_CUT = 18, 14


def kernel(
    nrow, ncol, slots, V,
    amp_ref, coul_ref, ilist_ref, icnt_ref, rlist_ref, rcnt_ref, virt_ref, occ_ref,
    out_ref,
    amps, coups, rows, coul, mirror, transit, state, acc, base, inv, wlin, wquad,
    ilist, icnt, rlist, rcnt, virt, occ,
    send_sem, recv_sem, load_sem,
):
    r = lax.axis_index("row")
    c = lax.axis_index("col")

    def flip(v, bit):
        return v + bit - 2 * bit * lax.rem(v // bit, 2)

    unit = 2 * V // 32

    def cut(parts):
        first, rest = parts * unit, (32 - parts) * unit
        return dict(
            p=pl.ds(0, first), pa=pl.ds(0, first // 2), pb=pl.ds(first // 2, first // 2),
            q=pl.ds(first, rest), qa=pl.ds(first, rest // 2),
            qb=pl.ds(first + rest // 2, rest // 2),
        )

    lin, quad = cut(LINEAR_CUT), cut(COUPLED_CUT)
    cuts = {0: lin, COL: quad}
    half_a, half_b = pl.ds(0, V), pl.ds(V, V)

    ry = flip(r, 1)
    rp, rm, r2 = lax.rem(r + 2, nrow), lax.rem(r + nrow - 2, nrow), lax.rem(r + 4, nrow)
    yp, ym, y2 = flip(rp, 1), flip(rm, 1), flip(r2, 1)
    ch, cs = flip(c, 2), flip(c, 1)
    cp, cm, c2 = lax.rem(c + 4, ncol), lax.rem(c + ncol - 4, ncol), lax.rem(c + 8, ncol)
    hp, hm, h2 = flip(cp, 2), flip(cm, 2), flip(c2, 2)
    to_y, to_right, to_left = (ry, c), (rp, c), (rm, c)
    to_n, to_zr, to_zl, to_s = (ry, ch), (r, cp), (r, cm), (r, cs)
    to_zrs, to_zls = (r, flip(cp, 1)), (r, flip(cm, 1))
    nx = nrow // 2
    x, lo = r // 2, lax.rem(r, 2)
    z, hi, core = c // 4, lax.rem(c // 2, 2), lax.rem(c, 2)
    ahead = lax.rem(z - x + nx, nx)

    def place(px, pz, plo, phi, pcore):
        return (
            2 * lax.rem(px + nx, nx) + plo, 4 * lax.rem(pz + nx, nx) + 2 * phi + pcore
        )

    step = 2 - ahead
    diagonal = ahead == 0
    opposite = ahead == 2
    beside = jnp.logical_or(ahead == 1, ahead == 3)
    mself = tuple(
        jnp.logical_and(diagonal, jnp.logical_and(lo == hi, core == a)) for a in range(2)
    )
    mout = tuple(jnp.logical_and(diagonal, jnp.logical_not(mself[a])) for a in range(2))

    loads = [
        pltpu.make_async_copy(amp_ref.at[a, 0], state.at[pl.ds(a * V, V)], load_sem.at[a])
        for a in range(2)
    ]
    for a in range(2):
        loads[a].start()
    coul_loads = [
        pltpu.make_async_copy(
            coul_ref.at[a], coul.at[:, pl.ds(a * V, V)], load_sem.at[2 + a]
        )
        for a in range(2)
    ]
    for a in range(2):
        coul_loads[a].start()
    small_loads = [
        pltpu.make_async_copy(src, dst, load_sem.at[4 + at])
        for at, (src, dst) in enumerate((
            (ilist_ref, ilist), (icnt_ref, icnt), (rlist_ref, rlist), (rcnt_ref, rcnt),
            (virt_ref, virt), (occ_ref, occ),
        ))
    ]
    for load in small_loads:
        load.start()

    barrier = pltpu.get_barrier_semaphore()
    for dev in (to_y, to_right, to_left, to_n, to_zr, to_zl, to_s, to_zrs, to_zls):
        pl.semaphore_signal(barrier, inc=1, device_id=dev, device_id_type=MESH)

    def greet(condition, *devices):
        @pl.when(condition)
        def _():
            for dev in devices:
                pl.semaphore_signal(barrier, inc=1, device_id=dev, device_id_type=MESH)

    greet(diagonal, place(x, z + 1, hi, lo, core), place(x, z - 1, hi, lo, core))
    for a in range(2):
        greet(mout[a], place(x, z, hi, lo, a))
        greet(jnp.logical_and(beside, core == 0), place(z, x, hi, lo, a))
        greet(jnp.logical_and(beside, core == 1), place(z, z, lo, hi, a))
        greet(jnp.logical_and(opposite, core == 0), place(x - 1, z, lo, hi, a))
        greet(jnp.logical_and(opposite, core == 1), place(x + 1, z, lo, hi, a))
    greet(beside, place(x - step, z, lo, hi, core), place(x, z + 2, hi, lo, core))
    for condition, count in (
        (jnp.logical_or(beside, jnp.logical_and(diagonal, lo != hi)), 13),
        (jnp.logical_and(diagonal, lo == hi), 12),
        (opposite, 11),
    ):
        @pl.when(condition)
        def _():
            pl.semaphore_wait(barrier, count)

    for a in range(2):
        loads[a].wait()

    def sweep(s, carry):
        def message(src, dst, key, dev, recv_key=None):
            return pltpu.make_async_remote_copy(
                src_ref=src, dst_ref=dst, send_sem=send_sem.at[s, key],
                recv_sem=recv_sem.at[s, key if recv_key is None else recv_key],
                device_id=dev, device_id_type=MESH,
            )

        def send(ref, key, dev):
            message(ref, ref, key, dev).start()

        def arrived(ref, key):
            message(ref, ref, key, to_y).wait_recv()

        def consume(left, weight, right, source, first=False):
            for b in range(2):
                orbital = 2 * source + b
                block = right[s, source, b * V:(b + 1) * V, :]
                for a in range(2):
                    at = slice(a * V, (a + 1) * V)
                    part = jnp.dot(left(orbital, a), block, preferred_element_type=F32)
                    part = part * weight[a, orbital]
                    if first and b == 0:
                        acc[at, :] = part
                    else:
                        acc[at, :] += part

        def open_q(buf, o):
            k = cuts[o]
            own = buf.at[s, r]
            send(own.at[k["p"]], o + Y_P, to_y)
            send(own.at[k["q"]], o + R_Q, to_right)
            send(own.at[k["q"]], o + L_Q, to_left)
            send(own.at[k["q"]], o + Y_Q, to_y)

        def open_p(buf, o):
            k = cuts[o]
            own = buf.at[s, r]
            send(own.at[k["p"]], o + R_P, to_right)
            send(own.at[k["p"]], o + L_P, to_left)

        def relay_q(buf, o):
            k = cuts[o]
            arrived(buf.at[s, rm, k["q"]], o + R_Q)
            send(buf.at[s, rm, k["qa"]], o + R_QA, to_right)
            send(buf.at[s, rm, k["q"]], o + Y_QM, to_y)
            arrived(buf.at[s, rp, k["q"]], o + L_Q)
            send(buf.at[s, rp, k["qb"]], o + L_QB, to_left)
            send(buf.at[s, rp, k["q"]], o + Y_QP, to_y)

        def relay_n(buf, o):
            k = cuts[o]
            arrived(buf.at[s, ry, k["p"]], o + Y_P)
            send(buf.at[s, ry, k["pa"]], o + R_NA, to_right)
            send(buf.at[s, ry, k["pb"]], o + L_NB, to_left)
            send(buf.at[s, ry, k["pb"]], o + R_NB, to_right)
            send(buf.at[s, ry, k["pa"]], o + L_NA, to_left)

        def relay_p(buf, o):
            k = cuts[o]
            arrived(buf.at[s, rm, k["p"]], o + R_P)
            send(buf.at[s, rm, k["pa"]], o + R_PA, to_right)
            arrived(buf.at[s, rp, k["p"]], o + L_P)
            send(buf.at[s, rp, k["pb"]], o + L_PB, to_left)

        def relay_q2(buf, o):
            k = cuts[o]
            arrived(buf.at[s, r2, k["qa"]], o + R_QA)
            send(buf.at[s, r2, k["qa"]], o + Y_Q2A, to_y)
            arrived(buf.at[s, r2, k["qb"]], o + L_QB)
            send(buf.at[s, r2, k["qb"]], o + Y_Q2B, to_y)

        def relay_nn(buf, o):
            k = cuts[o]
            arrived(buf.at[s, ym, k["pa"]], o + R_NA)
            send(buf.at[s, ym, k["pa"]], o + R_NRA, to_right)
            arrived(buf.at[s, yp, k["pb"]], o + L_NB)
            send(buf.at[s, yp, k["pb"]], o + L_NRB, to_left)
            arrived(buf.at[s, ym, k["pb"]], o + R_NB)
            arrived(buf.at[s, yp, k["pa"]], o + L_NA)

        def lin_left(orbital, a):
            return coul[orbital, a * V:(a + 1) * V, :]

        def quad_left(orbital, a):
            return rows[s, orbital, a * V:(a + 1) * V, :]

        start = state[...].astype(BF16)
        amps[s, r] = start
        rows[s, c] = start
        open_q(amps, 0)
        open_p(amps, 0)
        send(rows.at[s, c], ZR_O, to_zr)
        send(rows.at[s, c], ZL_O, to_zl)
        send(rows.at[s, c], S_O, to_s)

        @pl.when(s == 0)
        def _():
            for load in small_loads:
                load.wait()
            for weight, entries, count in (
                (wlin, lambda a, t: ilist[a, 0, t], lambda a: icnt[0, a]),
                (wquad, lambda a, t: rlist[a, t, c], lambda a: rcnt[a, c]),
            ):
                for a in range(2):
                    used = count(a)
                    listed = [jnp.where(t < used, entries(a, t), -1) for t in range(slots)]
                    for orbital in range(ncol):
                        hit = listed[0] == orbital
                        for t in range(1, slots):
                            hit = jnp.logical_or(hit, listed[t] == orbital)
                        weight[a, orbital] = jnp.where(hit, 1.0, 0.0).astype(F32)
            across = jnp.broadcast_to(virt[...], (V, V))
            pair = across + across.T
            for a in range(2):
                inv[a * V:(a + 1) * V, :] = 1.0 / (pair - occ[2 * r + a] - occ[c])
            for a in range(2):
                coul_loads[a].wait()

        consume(lin_left, wlin, amps, r, first=True)
        relay_q(amps, 0)
        relay_n(amps, 0)
        message(amps.at[s, ry, lin["p"]], rows.at[s, c, lin["p"]], N_P, to_n).start()
        relay_p(amps, 0)
        arrived(amps.at[s, ry, lin["q"]], Y_Q)
        message(amps.at[s, ry, lin["q"]], rows.at[s, c, lin["q"]], N_Q, to_n).start()
        arrived(rows.at[s, cm], ZR_O)
        send(rows.at[s, cm, half_a], ZR_OA, to_zr)
        send(rows.at[s, cm], S_M, to_s)
        arrived(rows.at[s, cp], ZL_O)
        send(rows.at[s, cp, half_b], ZL_OB, to_zl)
        send(rows.at[s, cp], S_P, to_s)
        consume(lin_left, wlin, amps, rm)
        relay_q2(amps, 0)
        consume(lin_left, wlin, amps, rp)
        consume(lin_left, wlin, amps, ry)
        arrived(rows.at[s, ch, lin["p"]], N_P)
        send(rows.at[s, ch, lin["p"]], ZR_HP, to_zr)
        send(rows.at[s, ch, lin["p"]], ZL_HP, to_zl)
        relay_nn(amps, 0)
        arrived(rows.at[s, ch, lin["q"]], N_Q)
        send(rows.at[s, ch, lin["q"]], ZR_HQ, to_zr)
        send(rows.at[s, ch, lin["q"]], ZL_HQ, to_zl)
        send(rows.at[s, ch], S_H, to_s)
        arrived(amps.at[s, ym, lin["q"]], Y_QM)
        consume(lin_left, wlin, amps, ym)
        arrived(amps.at[s, yp, lin["q"]], Y_QP)
        consume(lin_left, wlin, amps, yp)
        arrived(amps.at[s, r2, lin["pa"]], R_PA)
        arrived(amps.at[s, r2, lin["pb"]], L_PB)
        consume(lin_left, wlin, amps, r2)
        arrived(rows.at[s, c2, half_a], ZR_OA)
        arrived(rows.at[s, c2, half_b], ZL_OB)
        send(rows.at[s, c2], S_2, to_s)
        arrived(amps.at[s, y2, lin["qa"]], Y_Q2A)
        arrived(amps.at[s, y2, lin["qb"]], Y_Q2B)
        arrived(amps.at[s, y2, lin["pa"]], R_NRA)
        arrived(amps.at[s, y2, lin["pb"]], L_NRB)
        consume(lin_left, wlin, amps, y2)

        coups[s, r] = acc[...].astype(BF16)
        block = [coups.at[s, r, half_a], coups.at[s, r, half_b]]
        final = (mirror.at[s, core], M_0 + core)

        def forward(src, key, target, dev):
            message(src, target[0], key, dev, target[1]).start()

        @pl.when(opposite)
        def _():
            first = (transit.at[s, 0], X_0)
            forward(block[0], M_0, first, place(x + 1, z, lo, hi, core))
            forward(block[1], M_1, first, place(x - 1, z, lo, hi, core))


        open_q(coups, COL)
        open_p(coups, COL)

        @pl.when(beside)
        def _():
            crossing = ahead // 2
            forward(
                block[1], M_1, (transit.at[s, crossing], X_0 + crossing),
                place(x, x, hi, lo, core),
            )
            forward(block[0], M_0, final, place(z, x, hi, lo, 0))

        for a in range(2):
            @pl.when(mout[a])
            def _():
                forward(block[a], M_0 + a, final, place(x, z, hi, lo, a))

            @pl.when(mself[a])
            def _():
                mirror[s, a] = coups[s, r, a * V:(a + 1) * V, :]

        for a in range(2):
            at = slice(a * V, (a + 1) * V)
            linear = coul[c, at, :].astype(F32) + coupling * coups[s, r, at, :].astype(F32)
            base[at, :] = damping * state[at, :] - linear * inv[at, :]
        arrived(rows.at[s, hm, lin["p"]], ZR_HP)
        send(rows.at[s, hm, half_a], ZR_HA, to_zr)
        arrived(rows.at[s, hp, lin["p"]], ZL_HP)
        arrived(rows.at[s, hp, lin["q"]], ZL_HQ)
        send(rows.at[s, hp, half_b], ZL_HB, to_zl)
        arrived(rows.at[s, hm, lin["q"]], ZR_HQ)
        send(rows.at[s, hm], S_HM, to_s)
        send(rows.at[s, hp], S_HP, to_s)
        @pl.when(beside)
        def _():
            arrived(transit.at[s, 0], X_0)
            forward(
                transit.at[s, 0], X_0, (transit.at[s, 1], X_1), place(x, z + 2, hi, lo, core)
            )

        relay_q(coups, COL)
        relay_n(coups, COL)
        @pl.when(diagonal)
        def _():
            for at, px in ((0, x + 1), (1, x - 1)):
                arrived(transit.at[s, at], X_0 + at)
                forward(transit.at[s, at], X_0 + at, final, place(px, z, lo, hi, 1))

        arrived(rows.at[s, h2, half_a], ZR_HA)
        send(rows.at[s, h2, half_a], S_H2A, to_s)
        @pl.when(beside)
        def _():
            arrived(transit.at[s, 1], X_1)
            forward(transit.at[s, 1], X_1, final, place(x - step, z, lo, hi, ahead % 3))

        relay_p(coups, COL)
        arrived(rows.at[s, h2, half_b], ZL_HB)
        send(rows.at[s, h2, half_b], S_H2B, to_s)
        relay_q2(coups, COL)
        relay_nn(coups, COL)
        arrived(coups.at[s, ry, quad["q"]], COL + Y_Q)
        for own, key in (
            (c, S_O), (ch, S_H), (cm, S_M), (cp, S_P), (hm, S_HM), (hp, S_HP), (c2, S_2),
        ):
            arrived(rows.at[s, flip(own, 1)], key)
        arrived(rows.at[s, flip(h2, 1), half_a], S_H2A)
        arrived(rows.at[s, flip(h2, 1), half_b], S_H2B)
        consume(quad_left, wquad, coups, r, first=True)
        consume(quad_left, wquad, coups, rm)
        consume(quad_left, wquad, coups, rp)
        consume(quad_left, wquad, coups, ry)
        arrived(coups.at[s, ym, quad["q"]], COL + Y_QM)
        consume(quad_left, wquad, coups, ym)
        arrived(coups.at[s, yp, quad["q"]], COL + Y_QP)
        consume(quad_left, wquad, coups, yp)
        arrived(coups.at[s, r2, quad["pa"]], COL + R_PA)
        arrived(coups.at[s, r2, quad["pb"]], COL + L_PB)
        consume(quad_left, wquad, coups, r2)
        for a in range(2):
            @pl.when(jnp.logical_not(mself[a]))
            def _():
                arrived(mirror.at[s, a], M_0 + a)

            at = slice(a * V, (a + 1) * V)
            flipped = mirror[s, a].astype(F32).T
            base[at, :] -= coupling * flipped * inv[at, :]
        arrived(coups.at[s, y2, quad["qa"]], COL + Y_Q2A)
        arrived(coups.at[s, y2, quad["qb"]], COL + Y_Q2B)
        arrived(coups.at[s, y2, quad["pa"]], COL + R_NRA)
        arrived(coups.at[s, y2, quad["pb"]], COL + L_NRB)
        consume(quad_left, wquad, coups, y2)
        state[...] = base[...] - (coupling * coupling) * acc[...] * inv[...]
        return carry

    lax.fori_loop(0, ITERS, sweep, 0)
    for a in range(2):
        out_ref[a, 0] = state[a * V:(a + 1) * V, :]
    sizes = {}
    for o, k in cuts.items():
        for keys, part in (
            ((Y_P, R_P, L_P), "p"),
            ((Y_Q, Y_QM, Y_QP, R_Q, L_Q), "q"),
            ((Y_Q2A, Y_Q2B, R_QA, L_QB), "qa"),
            ((R_NA, R_NB, R_PA, R_NRA, L_NB, L_NA, L_PB, L_NRB), "pa"),
        ):
            for key in keys:
                sizes[o + key] = amps.at[0, r, k[part]]
    sizes[N_P], sizes[N_Q] = amps.at[0, r, lin["p"]], amps.at[0, r, lin["q"]]
    for part, keys in (("p", (ZR_HP, ZL_HP)), ("q", (ZR_HQ, ZL_HQ))):
        for key in keys:
            sizes[key] = rows.at[0, c, lin[part]]
    for key in (ZR_O, ZL_O, *range(S_O, S_H2A)):
        sizes[key] = rows.at[0, c]
    for key in (ZR_OA, ZR_HA, ZL_OB, ZL_HB, S_H2A, S_H2B):
        sizes[key] = rows.at[0, c, half_a]

    def drain(s, carry):
        def sent(ref, key):
            pltpu.make_async_remote_copy(
                src_ref=ref, dst_ref=ref, send_sem=send_sem.at[s, key],
                recv_sem=recv_sem.at[s, key], device_id=to_y, device_id_type=MESH,
            ).wait_send()

        for key, ref in sizes.items():
            sent(ref, key)
        for a in range(2):
            @pl.when(jnp.logical_not(mself[a]))
            def _():
                sent(mirror.at[0, a], M_0 + a)

        @pl.when(jnp.logical_not(opposite))
        def _():
            for a in range(2):
                sent(transit.at[0, a], X_0 + a)

        return carry

    lax.fori_loop(0, ITERS, drain, 0)


def on_device(
    amplitudes,
    coulomb,
    inner_list,
    inner_count,
    reader_list,
    reader_count,
    virtual_energy,
    occupied_energy,
    *,
    nrow,
    ncol,
):
    V = amplitudes.shape[2]
    slots = inner_list.shape[2]
    hbm = pl.BlockSpec(memory_space=pltpu.HBM)
    vmem = pl.BlockSpec(memory_space=pltpu.VMEM)
    return pl.pallas_call(
        functools.partial(kernel, nrow, ncol, slots, V),
        out_shape=pltpu.VMEM(amplitudes.shape, F32),
        in_specs=[hbm] * 8,
        out_specs=vmem,
        scratch_shapes=[
            pltpu.VMEM((ITERS, nrow, 2 * V, V), BF16),
            pltpu.VMEM((ITERS, nrow, 2 * V, V), BF16),
            pltpu.VMEM((ITERS, ncol, 2 * V, V), BF16),
            pltpu.VMEM((ncol, 2 * V, V), BF16),
            pltpu.VMEM((ITERS, 2, V, V), BF16),
            pltpu.VMEM((ITERS, 2, V, V), BF16),
            pltpu.VMEM((2 * V, V), F32),
            pltpu.VMEM((2 * V, V), F32),
            pltpu.VMEM((2 * V, V), F32),
            pltpu.VMEM((2 * V, V), F32),
            pltpu.SMEM((2, ncol), F32),
            pltpu.SMEM((2, ncol), F32),
            pltpu.SMEM((2, 1, slots), jnp.int32),
            pltpu.SMEM((1, 2), jnp.int32),
            pltpu.SMEM((2, slots, ncol), jnp.int32),
            pltpu.SMEM((2, ncol), jnp.int32),
            pltpu.VMEM((1, V), F32),
            pltpu.SMEM((ncol,), F32),
            pltpu.SemaphoreType.DMA((ITERS, COUNT)),
            pltpu.SemaphoreType.DMA((ITERS, COUNT)),
            pltpu.SemaphoreType.DMA((10,)),
        ],
        compiler_params=pltpu.CompilerParams(
            collective_id=0, has_side_effects=True, vmem_limit_bytes=66000000
        ),
        name="sweeps",
    )(
        amplitudes,
        coulomb,
        inner_list,
        inner_count.T,
        reader_list.transpose(0, 2, 1),
        reader_count,
        virtual_energy.reshape(1, V),
        occupied_energy,
    )


def solution(mesh):
    return jax.shard_map(
        functools.partial(on_device, nrow=mesh.shape["row"], ncol=mesh.shape["col"]),
        mesh=mesh,
        in_specs=(
            P("row", "col", None, None),
            P("row", None, None, None),
            P("row", "col", None),
            P("row", "col"),
            P("row", None, None),
            P("row", None),
            P(),
            P(),
        ),
        out_specs=P("row", "col", None, None),
        check_vma=False,
    )
```

```python
import functools

import jax
import jax.numpy as jnp
from jax import lax
from jax.experimental import pallas as pl
from jax.experimental.pallas import tpu as pltpu
from jax.sharding import PartitionSpec as P

ITERS = 2

damping = 0.5
coupling = 0.03125
MESH = pl.DeviceIdType.MESH
F32 = jnp.float32
BF16 = jnp.bfloat16

Y_P, Y_Q, Y_QM, Y_QP, Y_Q2A, Y_Q2B = range(6)
R_Q, R_P, R_QA, R_NA, R_NB, R_PA, R_NRA = range(6, 13)
L_Q, L_P, L_QB, L_NB, L_NA, L_PB, L_NRB = range(13, 20)
COL = 20
N_P, N_Q = 40, 41
ZR_O, ZR_HP, ZR_HQ, ZR_OA, ZR_HA = range(42, 47)
ZL_O, ZL_HP, ZL_HQ, ZL_OB, ZL_HB = range(47, 52)
S_O, S_H, S_M, S_P, S_HM, S_HP, S_2, S_H2A, S_H2B = range(52, 61)
M_0, M_1, X_0, X_1 = range(61, 65)
COUNT = 65
LINEAR_CUT, COUPLED_CUT = 18, 14


def kernel(
    nrow, ncol, slots, V,
    amp_ref, coul_ref, ilist_ref, icnt_ref, rlist_ref, rcnt_ref, virt_ref, occ_ref,
    out_ref,
    amps, coups, rows, coul, mirror, transit, state, acc, base, inv, wlin, wquad,
    ilist, icnt, rlist, rcnt, virt, occ,
    send_sem, recv_sem, load_sem,
):
    r = lax.axis_index("row")
    c = lax.axis_index("col")

    def flip(v, bit):
        return v + bit - 2 * bit * lax.rem(v // bit, 2)

    unit = 2 * V // 32

    def cut(parts):
        first, rest = parts * unit, (32 - parts) * unit
        return dict(
            p=pl.ds(0, first), pa=pl.ds(0, first // 2), pb=pl.ds(first // 2, first // 2),
            q=pl.ds(first, rest), qa=pl.ds(first, rest // 2),
            qb=pl.ds(first + rest // 2, rest // 2),
        )

    lin, quad = cut(LINEAR_CUT), cut(COUPLED_CUT)
    cuts = {0: lin, COL: quad}
    half_a, half_b = pl.ds(0, V), pl.ds(V, V)

    ry = flip(r, 1)
    rp, rm, r2 = lax.rem(r + 2, nrow), lax.rem(r + nrow - 2, nrow), lax.rem(r + 4, nrow)
    yp, ym, y2 = flip(rp, 1), flip(rm, 1), flip(r2, 1)
    ch, cs = flip(c, 2), flip(c, 1)
    cp, cm, c2 = lax.rem(c + 4, ncol), lax.rem(c + ncol - 4, ncol), lax.rem(c + 8, ncol)
    hp, hm, h2 = flip(cp, 2), flip(cm, 2), flip(c2, 2)
    to_y, to_right, to_left = (ry, c), (rp, c), (rm, c)
    to_n, to_zr, to_zl, to_s = (ry, ch), (r, cp), (r, cm), (r, cs)
    to_zrs, to_zls = (r, flip(cp, 1)), (r, flip(cm, 1))
    nx = nrow // 2
    x, lo = r // 2, lax.rem(r, 2)
    z, hi, core = c // 4, lax.rem(c // 2, 2), lax.rem(c, 2)
    ahead = lax.rem(z - x + nx, nx)

    def place(px, pz, plo, phi, pcore):
        return (
            2 * lax.rem(px + nx, nx) + plo, 4 * lax.rem(pz + nx, nx) + 2 * phi + pcore
        )

    step = 2 - ahead
    diagonal = ahead == 0
    opposite = ahead == 2
    beside = jnp.logical_or(ahead == 1, ahead == 3)
    mself = tuple(
        jnp.logical_and(diagonal, jnp.logical_and(lo == hi, core == a)) for a in range(2)
    )
    mout = tuple(jnp.logical_and(diagonal, jnp.logical_not(mself[a])) for a in range(2))

    loads = [
        pltpu.make_async_copy(amp_ref.at[a, 0], state.at[pl.ds(a * V, V)], load_sem.at[a])
        for a in range(2)
    ]
    for a in range(2):
        loads[a].start()
    coul_loads = [
        pltpu.make_async_copy(
            coul_ref.at[a], coul.at[:, pl.ds(a * V, V)], load_sem.at[2 + a]
        )
        for a in range(2)
    ]
    for a in range(2):
        coul_loads[a].start()
    small_loads = [
        pltpu.make_async_copy(src, dst, load_sem.at[4 + at])
        for at, (src, dst) in enumerate((
            (ilist_ref, ilist), (icnt_ref, icnt), (rlist_ref, rlist), (rcnt_ref, rcnt),
            (virt_ref, virt), (occ_ref, occ),
        ))
    ]
    for load in small_loads:
        load.start()

    barrier = pltpu.get_barrier_semaphore()
    for dev in (to_y, to_right, to_left, to_n, to_zr, to_zl, to_s, to_zrs, to_zls):
        pl.semaphore_signal(barrier, inc=1, device_id=dev, device_id_type=MESH)

    def greet(condition, *devices):
        @pl.when(condition)
        def _():
            for dev in devices:
                pl.semaphore_signal(barrier, inc=1, device_id=dev, device_id_type=MESH)

    greet(diagonal, place(x, z + 1, hi, lo, core), place(x, z - 1, hi, lo, core))
    for a in range(2):
        greet(mout[a], place(x, z, hi, lo, a))
        greet(jnp.logical_and(beside, core == 0), place(z, x, hi, lo, a))
        greet(jnp.logical_and(beside, core == 1), place(z, z, lo, hi, a))
        greet(jnp.logical_and(opposite, core == 0), place(x - 1, z, lo, hi, a))
        greet(jnp.logical_and(opposite, core == 1), place(x + 1, z, lo, hi, a))
    greet(beside, place(x - step, z, lo, hi, core), place(x, z + 2, hi, lo, core))
    for condition, count in (
        (jnp.logical_or(beside, jnp.logical_and(diagonal, lo != hi)), 13),
        (jnp.logical_and(diagonal, lo == hi), 12),
        (opposite, 11),
    ):
        @pl.when(condition)
        def _():
            pl.semaphore_wait(barrier, count)

    for a in range(2):
        loads[a].wait()

    sizes = {}
    for o, k in cuts.items():
        for keys, part in (
            ((Y_P, R_P, L_P), "p"),
            ((Y_Q, Y_QM, Y_QP, R_Q, L_Q), "q"),
            ((Y_Q2A, Y_Q2B, R_QA, L_QB), "qa"),
            ((R_NA, R_NB, R_PA, R_NRA, L_NB, L_NA, L_PB, L_NRB), "pa"),
        ):
            for key in keys:
                sizes[o + key] = amps.at[0, r, k[part]]
    sizes[N_P], sizes[N_Q] = amps.at[0, r, lin["p"]], amps.at[0, r, lin["q"]]
    for part, keys in (("p", (ZR_HP, ZL_HP)), ("q", (ZR_HQ, ZL_HQ))):
        for key in keys:
            sizes[key] = rows.at[0, c, lin[part]]
    for key in (ZR_O, ZL_O, *range(S_O, S_H2A)):
        sizes[key] = rows.at[0, c]
    for key in (ZR_OA, ZR_HA, ZL_OB, ZL_HB, S_H2A, S_H2B):
        sizes[key] = rows.at[0, c, half_a]

    def drain(s, carry):
        def sent(ref, key):
            pltpu.make_async_remote_copy(
                src_ref=ref, dst_ref=ref, send_sem=send_sem.at[s, key],
                recv_sem=recv_sem.at[s, key], device_id=to_y, device_id_type=MESH,
            ).wait_send()

        for key, ref in sizes.items():
            sent(ref, key)
        for a in range(2):
            @pl.when(jnp.logical_not(mself[a]))
            def _():
                sent(mirror.at[0, a], M_0 + a)

        @pl.when(jnp.logical_not(opposite))
        def _():
            for a in range(2):
                sent(transit.at[0, a], X_0 + a)

        return carry

    def sweep(s, carry):
        def message(src, dst, key, dev, recv_key=None):
            return pltpu.make_async_remote_copy(
                src_ref=src, dst_ref=dst, send_sem=send_sem.at[s, key],
                recv_sem=recv_sem.at[s, key if recv_key is None else recv_key],
                device_id=dev, device_id_type=MESH,
            )

        def send(ref, key, dev):
            message(ref, ref, key, dev).start()

        def arrived(ref, key):
            message(ref, ref, key, to_y).wait_recv()

        def consume(left, weight, right, source, first=False):
            for b in range(2):
                orbital = 2 * source + b
                block = right[s, source, b * V:(b + 1) * V, :]
                for a in range(2):
                    at = slice(a * V, (a + 1) * V)
                    part = jnp.dot(left(orbital, a), block, preferred_element_type=F32)
                    part = part * weight[a, orbital]
                    if first and b == 0:
                        acc[at, :] = part
                    else:
                        acc[at, :] += part

        def open_q(buf, o):
            k = cuts[o]
            own = buf.at[s, r]
            send(own.at[k["p"]], o + Y_P, to_y)
            send(own.at[k["q"]], o + R_Q, to_right)
            send(own.at[k["q"]], o + L_Q, to_left)
            send(own.at[k["q"]], o + Y_Q, to_y)

        def open_p(buf, o):
            k = cuts[o]
            own = buf.at[s, r]
            send(own.at[k["p"]], o + R_P, to_right)
            send(own.at[k["p"]], o + L_P, to_left)

        def relay_q(buf, o):
            k = cuts[o]
            arrived(buf.at[s, rm, k["q"]], o + R_Q)
            send(buf.at[s, rm, k["qa"]], o + R_QA, to_right)
            send(buf.at[s, rm, k["q"]], o + Y_QM, to_y)
            arrived(buf.at[s, rp, k["q"]], o + L_Q)
            send(buf.at[s, rp, k["qb"]], o + L_QB, to_left)
            send(buf.at[s, rp, k["q"]], o + Y_QP, to_y)

        def relay_n(buf, o):
            k = cuts[o]
            arrived(buf.at[s, ry, k["p"]], o + Y_P)
            send(buf.at[s, ry, k["pa"]], o + R_NA, to_right)
            send(buf.at[s, ry, k["pb"]], o + L_NB, to_left)
            send(buf.at[s, ry, k["pb"]], o + R_NB, to_right)
            send(buf.at[s, ry, k["pa"]], o + L_NA, to_left)

        def relay_p(buf, o):
            k = cuts[o]
            arrived(buf.at[s, rm, k["p"]], o + R_P)
            send(buf.at[s, rm, k["pa"]], o + R_PA, to_right)
            arrived(buf.at[s, rp, k["p"]], o + L_P)
            send(buf.at[s, rp, k["pb"]], o + L_PB, to_left)

        def relay_q2(buf, o):
            k = cuts[o]
            arrived(buf.at[s, r2, k["qa"]], o + R_QA)
            send(buf.at[s, r2, k["qa"]], o + Y_Q2A, to_y)
            arrived(buf.at[s, r2, k["qb"]], o + L_QB)
            send(buf.at[s, r2, k["qb"]], o + Y_Q2B, to_y)

        def relay_nn(buf, o):
            k = cuts[o]
            arrived(buf.at[s, ym, k["pa"]], o + R_NA)
            send(buf.at[s, ym, k["pa"]], o + R_NRA, to_right)
            arrived(buf.at[s, yp, k["pb"]], o + L_NB)
            send(buf.at[s, yp, k["pb"]], o + L_NRB, to_left)
            arrived(buf.at[s, ym, k["pb"]], o + R_NB)
            arrived(buf.at[s, yp, k["pa"]], o + L_NA)

        def lin_left(orbital, a):
            return coul[orbital, a * V:(a + 1) * V, :]

        def quad_left(orbital, a):
            return rows[s, orbital, a * V:(a + 1) * V, :]

        start = state[...].astype(BF16)
        amps[s, r] = start
        rows[s, c] = start
        open_q(amps, 0)
        open_p(amps, 0)
        send(rows.at[s, c], ZR_O, to_zr)
        send(rows.at[s, c], ZL_O, to_zl)
        send(rows.at[s, c], S_O, to_s)

        @pl.when(s == 0)
        def _():
            for load in small_loads:
                load.wait()
            for weight, entries, count in (
                (wlin, lambda a, t: ilist[a, 0, t], lambda a: icnt[0, a]),
                (wquad, lambda a, t: rlist[a, t, c], lambda a: rcnt[a, c]),
            ):
                for a in range(2):
                    used = count(a)
                    listed = [jnp.where(t < used, entries(a, t), -1) for t in range(slots)]
                    for orbital in range(ncol):
                        hit = listed[0] == orbital
                        for t in range(1, slots):
                            hit = jnp.logical_or(hit, listed[t] == orbital)
                        weight[a, orbital] = jnp.where(hit, 1.0, 0.0).astype(F32)
            across = jnp.broadcast_to(virt[...], (V, V))
            pair = across + across.T
            for a in range(2):
                inv[a * V:(a + 1) * V, :] = 1.0 / (pair - occ[2 * r + a] - occ[c])
            for a in range(2):
                coul_loads[a].wait()

        consume(lin_left, wlin, amps, r, first=True)

        @pl.when(s > 0)
        def _():
            drain(s - 1, 0)

        relay_q(amps, 0)
        relay_n(amps, 0)
        message(amps.at[s, ry, lin["p"]], rows.at[s, c, lin["p"]], N_P, to_n).start()
        relay_p(amps, 0)
        arrived(amps.at[s, ry, lin["q"]], Y_Q)
        message(amps.at[s, ry, lin["q"]], rows.at[s, c, lin["q"]], N_Q, to_n).start()
        arrived(rows.at[s, cm], ZR_O)
        send(rows.at[s, cm, half_a], ZR_OA, to_zr)
        send(rows.at[s, cm], S_M, to_s)
        arrived(rows.at[s, cp], ZL_O)
        send(rows.at[s, cp, half_b], ZL_OB, to_zl)
        send(rows.at[s, cp], S_P, to_s)
        relay_q2(amps, 0)
        consume(lin_left, wlin, amps, rm)
        consume(lin_left, wlin, amps, rp)
        consume(lin_left, wlin, amps, ry)
        arrived(rows.at[s, ch, lin["p"]], N_P)
        send(rows.at[s, ch, lin["p"]], ZR_HP, to_zr)
        send(rows.at[s, ch, lin["p"]], ZL_HP, to_zl)
        relay_nn(amps, 0)
        arrived(rows.at[s, ch, lin["q"]], N_Q)
        send(rows.at[s, ch, lin["q"]], ZR_HQ, to_zr)
        send(rows.at[s, ch, lin["q"]], ZL_HQ, to_zl)
        send(rows.at[s, ch], S_H, to_s)
        arrived(amps.at[s, ym, lin["q"]], Y_QM)
        consume(lin_left, wlin, amps, ym)
        arrived(amps.at[s, yp, lin["q"]], Y_QP)
        consume(lin_left, wlin, amps, yp)
        arrived(amps.at[s, r2, lin["pa"]], R_PA)
        arrived(amps.at[s, r2, lin["pb"]], L_PB)
        consume(lin_left, wlin, amps, r2)
        arrived(rows.at[s, c2, half_a], ZR_OA)
        arrived(rows.at[s, c2, half_b], ZL_OB)
        send(rows.at[s, c2], S_2, to_s)
        arrived(amps.at[s, y2, lin["qa"]], Y_Q2A)
        arrived(amps.at[s, y2, lin["qb"]], Y_Q2B)
        arrived(amps.at[s, y2, lin["pa"]], R_NRA)
        arrived(amps.at[s, y2, lin["pb"]], L_NRB)
        consume(lin_left, wlin, amps, y2)

        coups[s, r] = acc[...].astype(BF16)
        block = [coups.at[s, r, half_a], coups.at[s, r, half_b]]
        final = (mirror.at[s, core], M_0 + core)

        def forward(src, key, target, dev):
            message(src, target[0], key, dev, target[1]).start()

        @pl.when(opposite)
        def _():
            first = (transit.at[s, 0], X_0)
            forward(block[0], M_0, first, place(x + 1, z, lo, hi, core))
            forward(block[1], M_1, first, place(x - 1, z, lo, hi, core))


        open_q(coups, COL)
        open_p(coups, COL)

        @pl.when(beside)
        def _():
            crossing = ahead // 2
            forward(
                block[1], M_1, (transit.at[s, crossing], X_0 + crossing),
                place(x, x, hi, lo, core),
            )
            forward(block[0], M_0, final, place(z, x, hi, lo, 0))

        for a in range(2):
            @pl.when(mout[a])
            def _():
                forward(block[a], M_0 + a, final, place(x, z, hi, lo, a))

            @pl.when(mself[a])
            def _():
                mirror[s, a] = coups[s, r, a * V:(a + 1) * V, :]

        for a in range(2):
            at = slice(a * V, (a + 1) * V)
            linear = coul[c, at, :].astype(F32) + coupling * coups[s, r, at, :].astype(F32)
            base[at, :] = damping * state[at, :] - linear * inv[at, :]
        arrived(rows.at[s, hm, lin["p"]], ZR_HP)
        send(rows.at[s, hm, half_a], ZR_HA, to_zr)
        arrived(rows.at[s, hp, lin["p"]], ZL_HP)
        arrived(rows.at[s, hp, lin["q"]], ZL_HQ)
        send(rows.at[s, hp, half_b], ZL_HB, to_zl)
        arrived(rows.at[s, hm, lin["q"]], ZR_HQ)
        send(rows.at[s, hm], S_HM, to_s)
        send(rows.at[s, hp], S_HP, to_s)
        @pl.when(beside)
        def _():
            arrived(transit.at[s, 0], X_0)
            forward(
                transit.at[s, 0], X_0, (transit.at[s, 1], X_1), place(x, z + 2, hi, lo, core)
            )

        relay_q(coups, COL)
        relay_n(coups, COL)
        @pl.when(diagonal)
        def _():
            for at, px in ((0, x + 1), (1, x - 1)):
                arrived(transit.at[s, at], X_0 + at)
                forward(transit.at[s, at], X_0 + at, final, place(px, z, lo, hi, 1))

        arrived(rows.at[s, h2, half_a], ZR_HA)
        send(rows.at[s, h2, half_a], S_H2A, to_s)
        @pl.when(beside)
        def _():
            arrived(transit.at[s, 1], X_1)
            forward(transit.at[s, 1], X_1, final, place(x - step, z, lo, hi, ahead % 3))

        relay_p(coups, COL)
        arrived(rows.at[s, h2, half_b], ZL_HB)
        send(rows.at[s, h2, half_b], S_H2B, to_s)
        relay_q2(coups, COL)
        relay_nn(coups, COL)
        arrived(coups.at[s, ry, quad["q"]], COL + Y_Q)
        for own, key in (
            (c, S_O), (ch, S_H), (cm, S_M), (cp, S_P), (hm, S_HM), (hp, S_HP), (c2, S_2),
        ):
            arrived(rows.at[s, flip(own, 1)], key)
        arrived(rows.at[s, flip(h2, 1), half_a], S_H2A)
        arrived(rows.at[s, flip(h2, 1), half_b], S_H2B)
        consume(quad_left, wquad, coups, r, first=True)
        consume(quad_left, wquad, coups, rm)
        consume(quad_left, wquad, coups, rp)
        consume(quad_left, wquad, coups, ry)
        arrived(coups.at[s, ym, quad["q"]], COL + Y_QM)
        consume(quad_left, wquad, coups, ym)
        arrived(coups.at[s, yp, quad["q"]], COL + Y_QP)
        consume(quad_left, wquad, coups, yp)
        arrived(coups.at[s, r2, quad["pa"]], COL + R_PA)
        arrived(coups.at[s, r2, quad["pb"]], COL + L_PB)
        consume(quad_left, wquad, coups, r2)
        for a in range(2):
            @pl.when(jnp.logical_not(mself[a]))
            def _():
                arrived(mirror.at[s, a], M_0 + a)

            at = slice(a * V, (a + 1) * V)
            flipped = mirror[s, a].astype(F32).T
            base[at, :] -= coupling * flipped * inv[at, :]
        arrived(coups.at[s, y2, quad["qa"]], COL + Y_Q2A)
        arrived(coups.at[s, y2, quad["qb"]], COL + Y_Q2B)
        arrived(coups.at[s, y2, quad["pa"]], COL + R_NRA)
        arrived(coups.at[s, y2, quad["pb"]], COL + L_NRB)
        consume(quad_left, wquad, coups, y2)
        state[...] = base[...] - (coupling * coupling) * acc[...] * inv[...]
        return carry

    lax.fori_loop(0, ITERS, sweep, 0)
    for a in range(2):
        out_ref[a, 0] = state[a * V:(a + 1) * V, :]
    drain(ITERS - 1, 0)


def on_device(
    amplitudes,
    coulomb,
    inner_list,
    inner_count,
    reader_list,
    reader_count,
    virtual_energy,
    occupied_energy,
    *,
    nrow,
    ncol,
):
    V = amplitudes.shape[2]
    slots = inner_list.shape[2]
    hbm = pl.BlockSpec(memory_space=pltpu.HBM)
    vmem = pl.BlockSpec(memory_space=pltpu.VMEM)
    return pl.pallas_call(
        functools.partial(kernel, nrow, ncol, slots, V),
        out_shape=pltpu.VMEM(amplitudes.shape, F32),
        in_specs=[hbm] * 8,
        out_specs=vmem,
        scratch_shapes=[
            pltpu.VMEM((ITERS, nrow, 2 * V, V), BF16),
            pltpu.VMEM((ITERS, nrow, 2 * V, V), BF16),
            pltpu.VMEM((ITERS, ncol, 2 * V, V), BF16),
            pltpu.VMEM((ncol, 2 * V, V), BF16),
            pltpu.VMEM((ITERS, 2, V, V), BF16),
            pltpu.VMEM((ITERS, 2, V, V), BF16),
            pltpu.VMEM((2 * V, V), F32),
            pltpu.VMEM((2 * V, V), F32),
            pltpu.VMEM((2 * V, V), F32),
            pltpu.VMEM((2 * V, V), F32),
            pltpu.SMEM((2, ncol), F32),
            pltpu.SMEM((2, ncol), F32),
            pltpu.SMEM((2, 1, slots), jnp.int32),
            pltpu.SMEM((1, 2), jnp.int32),
            pltpu.SMEM((2, slots, ncol), jnp.int32),
            pltpu.SMEM((2, ncol), jnp.int32),
            pltpu.VMEM((1, V), F32),
            pltpu.SMEM((ncol,), F32),
            pltpu.SemaphoreType.DMA((ITERS, COUNT)),
            pltpu.SemaphoreType.DMA((ITERS, COUNT)),
            pltpu.SemaphoreType.DMA((10,)),
        ],
        compiler_params=pltpu.CompilerParams(
            collective_id=0, has_side_effects=True, vmem_limit_bytes=66000000
        ),
        name="sweeps",
    )(
        amplitudes,
        coulomb,
        inner_list,
        inner_count.T,
        reader_list.transpose(0, 2, 1),
        reader_count,
        virtual_energy.reshape(1, V),
        occupied_energy,
    )


def solution(mesh):
    return jax.shard_map(
        functools.partial(on_device, nrow=mesh.shape["row"], ncol=mesh.shape["col"]),
        mesh=mesh,
        in_specs=(
            P("row", "col", None, None),
            P("row", None, None, None),
            P("row", "col", None),
            P("row", "col"),
            P("row", None, None),
            P("row", None),
            P(),
            P(),
        ),
        out_specs=P("row", "col", None, None),
        check_vma=False,
    )
```

```python
import functools

import jax
import jax.numpy as jnp
from jax import lax
from jax.experimental import pallas as pl
from jax.experimental.pallas import tpu as pltpu
from jax.sharding import PartitionSpec as P

ITERS = 2

damping = 0.5
coupling = 0.03125
MESH = pl.DeviceIdType.MESH
F32 = jnp.float32
BF16 = jnp.bfloat16

Y_P, Y_Q, Y_QM, Y_QP, Y_Q2A, Y_Q2B = range(6)
R_Q, R_P, R_QA, R_NA, R_NB, R_PA, R_NRA = range(6, 13)
L_Q, L_P, L_QB, L_NB, L_NA, L_PB, L_NRB = range(13, 20)
COL = 20
N_P, N_Q = 40, 41
ZR_O, ZR_HP, ZR_HQ, ZR_OA, ZR_HA = range(42, 47)
ZL_O, ZL_HP, ZL_HQ, ZL_OB, ZL_HB = range(47, 52)
S_O, S_H, S_M, S_P, S_HM, S_HP, S_2, S_H2A, S_H2B = range(52, 61)
M_0, M_1, X_0, X_1 = range(61, 65)
COUNT = 65
LINEAR_CUT, COUPLED_CUT = 18, 14


def kernel(
    nrow, ncol, slots, V,
    amp_ref, coul_ref, ilist_ref, icnt_ref, rlist_ref, rcnt_ref, virt_ref, occ_ref,
    out_ref,
    amps, coups, rows, coul, mirror, transit, state, acc, base, inv, wlin, wquad,
    ilist, icnt, rlist, rcnt, virt, occ,
    send_sem, recv_sem, load_sem,
):
    r = lax.axis_index("row")
    c = lax.axis_index("col")

    def flip(v, bit):
        return v + bit - 2 * bit * lax.rem(v // bit, 2)

    unit = 2 * V // 32

    def cut(parts):
        first, rest = parts * unit, (32 - parts) * unit
        return dict(
            p=pl.ds(0, first), pa=pl.ds(0, first // 2), pb=pl.ds(first // 2, first // 2),
            q=pl.ds(first, rest), qa=pl.ds(first, rest // 2),
            qb=pl.ds(first + rest // 2, rest // 2),
        )

    lin, quad = cut(LINEAR_CUT), cut(COUPLED_CUT)
    cuts = {0: lin, COL: quad}
    half_a, half_b = pl.ds(0, V), pl.ds(V, V)

    ry = flip(r, 1)
    rp, rm, r2 = lax.rem(r + 2, nrow), lax.rem(r + nrow - 2, nrow), lax.rem(r + 4, nrow)
    yp, ym, y2 = flip(rp, 1), flip(rm, 1), flip(r2, 1)
    ch, cs = flip(c, 2), flip(c, 1)
    cp, cm, c2 = lax.rem(c + 4, ncol), lax.rem(c + ncol - 4, ncol), lax.rem(c + 8, ncol)
    hp, hm, h2 = flip(cp, 2), flip(cm, 2), flip(c2, 2)
    to_y, to_right, to_left = (ry, c), (rp, c), (rm, c)
    to_n, to_zr, to_zl, to_s = (ry, ch), (r, cp), (r, cm), (r, cs)
    to_zrs, to_zls = (r, flip(cp, 1)), (r, flip(cm, 1))
    nx = nrow // 2
    x, lo = r // 2, lax.rem(r, 2)
    z, hi, core = c // 4, lax.rem(c // 2, 2), lax.rem(c, 2)
    ahead = lax.rem(z - x + nx, nx)

    def place(px, pz, plo, phi, pcore):
        return (
            2 * lax.rem(px + nx, nx) + plo, 4 * lax.rem(pz + nx, nx) + 2 * phi + pcore
        )

    step = 2 - ahead
    diagonal = ahead == 0
    opposite = ahead == 2
    beside = jnp.logical_or(ahead == 1, ahead == 3)
    mself = tuple(
        jnp.logical_and(diagonal, jnp.logical_and(lo == hi, core == a)) for a in range(2)
    )
    mout = tuple(jnp.logical_and(diagonal, jnp.logical_not(mself[a])) for a in range(2))

    loads = [
        pltpu.make_async_copy(amp_ref.at[a, 0], state.at[pl.ds(a * V, V)], load_sem.at[a])
        for a in range(2)
    ]
    for a in range(2):
        loads[a].start()
    coul_loads = [
        pltpu.make_async_copy(
            coul_ref.at[a], coul.at[:, pl.ds(a * V, V)], load_sem.at[2 + a]
        )
        for a in range(2)
    ]
    for a in range(2):
        coul_loads[a].start()
    small_loads = [
        pltpu.make_async_copy(src, dst, load_sem.at[4 + at])
        for at, (src, dst) in enumerate((
            (ilist_ref, ilist), (icnt_ref, icnt), (rlist_ref, rlist), (rcnt_ref, rcnt),
            (virt_ref, virt), (occ_ref, occ),
        ))
    ]
    for load in small_loads:
        load.start()

    barrier = pltpu.get_barrier_semaphore()
    for dev in (to_y, to_right, to_left, to_n, to_zr, to_zl, to_s, to_zrs, to_zls):
        pl.semaphore_signal(barrier, inc=1, device_id=dev, device_id_type=MESH)

    def greet(condition, *devices):
        @pl.when(condition)
        def _():
            for dev in devices:
                pl.semaphore_signal(barrier, inc=1, device_id=dev, device_id_type=MESH)

    greet(diagonal, place(x, z + 1, hi, lo, core), place(x, z - 1, hi, lo, core))
    for a in range(2):
        greet(mout[a], place(x, z, hi, lo, a))
        greet(jnp.logical_and(beside, core == 0), place(z, x, hi, lo, a))
        greet(jnp.logical_and(beside, core == 1), place(z, z, lo, hi, a))
        greet(jnp.logical_and(opposite, core == 0), place(x - 1, z, lo, hi, a))
        greet(jnp.logical_and(opposite, core == 1), place(x + 1, z, lo, hi, a))
    greet(beside, place(x - step, z, lo, hi, core), place(x, z + 2, hi, lo, core))
    for condition, count in (
        (jnp.logical_or(beside, jnp.logical_and(diagonal, lo != hi)), 13),
        (jnp.logical_and(diagonal, lo == hi), 12),
        (opposite, 11),
    ):
        @pl.when(condition)
        def _():
            pl.semaphore_wait(barrier, count)

    for a in range(2):
        loads[a].wait()

    def sweep(s, carry):
        def message(src, dst, key, dev, recv_key=None):
            return pltpu.make_async_remote_copy(
                src_ref=src, dst_ref=dst, send_sem=send_sem.at[s, key],
                recv_sem=recv_sem.at[s, key if recv_key is None else recv_key],
                device_id=dev, device_id_type=MESH,
            )

        def send(ref, key, dev):
            message(ref, ref, key, dev).start()

        def arrived(ref, key):
            message(ref, ref, key, to_y).wait_recv()

        def consume(left, weight, right, source, first=False):
            for b in range(2):
                orbital = 2 * source + b
                block = right[s, source, b * V:(b + 1) * V, :]
                for a in range(2):
                    at = slice(a * V, (a + 1) * V)
                    part = jnp.dot(left(orbital, a), block, preferred_element_type=F32)
                    part = part * weight[a, orbital]
                    if first and b == 0:
                        acc[at, :] = part
                    else:
                        acc[at, :] += part

        def open_q(buf, o):
            k = cuts[o]
            own = buf.at[s, r]
            send(own.at[k["p"]], o + Y_P, to_y)
            send(own.at[k["q"]], o + R_Q, to_right)
            send(own.at[k["q"]], o + L_Q, to_left)
            send(own.at[k["q"]], o + Y_Q, to_y)

        def open_p(buf, o):
            k = cuts[o]
            own = buf.at[s, r]
            send(own.at[k["p"]], o + R_P, to_right)
            send(own.at[k["p"]], o + L_P, to_left)

        def relay_q(buf, o):
            k = cuts[o]
            arrived(buf.at[s, rm, k["q"]], o + R_Q)
            send(buf.at[s, rm, k["qa"]], o + R_QA, to_right)
            send(buf.at[s, rm, k["q"]], o + Y_QM, to_y)
            arrived(buf.at[s, rp, k["q"]], o + L_Q)
            send(buf.at[s, rp, k["qb"]], o + L_QB, to_left)
            send(buf.at[s, rp, k["q"]], o + Y_QP, to_y)

        def relay_n(buf, o):
            k = cuts[o]
            arrived(buf.at[s, ry, k["p"]], o + Y_P)
            send(buf.at[s, ry, k["pa"]], o + R_NA, to_right)
            send(buf.at[s, ry, k["pb"]], o + L_NB, to_left)
            send(buf.at[s, ry, k["pb"]], o + R_NB, to_right)
            send(buf.at[s, ry, k["pa"]], o + L_NA, to_left)

        def relay_p(buf, o):
            k = cuts[o]
            arrived(buf.at[s, rm, k["p"]], o + R_P)
            send(buf.at[s, rm, k["pa"]], o + R_PA, to_right)
            arrived(buf.at[s, rp, k["p"]], o + L_P)
            send(buf.at[s, rp, k["pb"]], o + L_PB, to_left)

        def relay_q2(buf, o):
            k = cuts[o]
            arrived(buf.at[s, r2, k["qa"]], o + R_QA)
            send(buf.at[s, r2, k["qa"]], o + Y_Q2A, to_y)
            arrived(buf.at[s, r2, k["qb"]], o + L_QB)
            send(buf.at[s, r2, k["qb"]], o + Y_Q2B, to_y)

        def relay_nn(buf, o):
            k = cuts[o]
            arrived(buf.at[s, ym, k["pa"]], o + R_NA)
            send(buf.at[s, ym, k["pa"]], o + R_NRA, to_right)
            arrived(buf.at[s, yp, k["pb"]], o + L_NB)
            send(buf.at[s, yp, k["pb"]], o + L_NRB, to_left)
            arrived(buf.at[s, ym, k["pb"]], o + R_NB)
            arrived(buf.at[s, yp, k["pa"]], o + L_NA)

        def lin_left(orbital, a):
            return coul[orbital, a * V:(a + 1) * V, :]

        def quad_left(orbital, a):
            return rows[s, orbital, a * V:(a + 1) * V, :]

        start = state[...].astype(BF16)
        amps[s, r] = start
        rows[s, c] = start
        open_q(amps, 0)
        open_p(amps, 0)
        send(rows.at[s, c], ZR_O, to_zr)
        send(rows.at[s, c], ZL_O, to_zl)
        send(rows.at[s, c], S_O, to_s)

        @pl.when(s == 0)
        def _():
            for load in small_loads:
                load.wait()
            for weight, entries, count in (
                (wlin, lambda a, t: ilist[a, 0, t], lambda a: icnt[0, a]),
                (wquad, lambda a, t: rlist[a, t, c], lambda a: rcnt[a, c]),
            ):
                for a in range(2):
                    used = count(a)
                    listed = [jnp.where(t < used, entries(a, t), -1) for t in range(slots)]
                    for orbital in range(ncol):
                        hit = listed[0] == orbital
                        for t in range(1, slots):
                            hit = jnp.logical_or(hit, listed[t] == orbital)
                        weight[a, orbital] = jnp.where(hit, 1.0, 0.0).astype(F32)
            across = jnp.broadcast_to(virt[...], (V, V))
            pair = across + across.T
            for a in range(2):
                inv[a * V:(a + 1) * V, :] = 1.0 / (pair - occ[2 * r + a] - occ[c])
            for a in range(2):
                coul_loads[a].wait()

        consume(lin_left, wlin, amps, r, first=True)
        relay_q(amps, 0)
        relay_n(amps, 0)
        message(amps.at[s, ry, lin["p"]], rows.at[s, c, lin["p"]], N_P, to_n).start()
        relay_p(amps, 0)
        arrived(amps.at[s, ry, lin["q"]], Y_Q)
        message(amps.at[s, ry, lin["q"]], rows.at[s, c, lin["q"]], N_Q, to_n).start()
        arrived(rows.at[s, cm], ZR_O)
        send(rows.at[s, cm, half_a], ZR_OA, to_zr)
        send(rows.at[s, cm], S_M, to_s)
        arrived(rows.at[s, cp], ZL_O)
        send(rows.at[s, cp, half_b], ZL_OB, to_zl)
        send(rows.at[s, cp], S_P, to_s)
        consume(lin_left, wlin, amps, rm)
        relay_q2(amps, 0)
        consume(lin_left, wlin, amps, rp)
        consume(lin_left, wlin, amps, ry)
        arrived(rows.at[s, ch, lin["p"]], N_P)
        send(rows.at[s, ch, lin["p"]], ZR_HP, to_zr)
        send(rows.at[s, ch, lin["p"]], ZL_HP, to_zl)
        relay_nn(amps, 0)
        arrived(rows.at[s, ch, lin["q"]], N_Q)
        send(rows.at[s, ch, lin["q"]], ZR_HQ, to_zr)
        send(rows.at[s, ch, lin["q"]], ZL_HQ, to_zl)
        send(rows.at[s, ch], S_H, to_s)
        arrived(amps.at[s, ym, lin["q"]], Y_QM)
        consume(lin_left, wlin, amps, ym)
        arrived(amps.at[s, yp, lin["q"]], Y_QP)
        consume(lin_left, wlin, amps, yp)
        arrived(amps.at[s, r2, lin["pa"]], R_PA)
        arrived(amps.at[s, r2, lin["pb"]], L_PB)
        consume(lin_left, wlin, amps, r2)
        arrived(rows.at[s, c2, half_a], ZR_OA)
        arrived(rows.at[s, c2, half_b], ZL_OB)
        send(rows.at[s, c2], S_2, to_s)
        arrived(amps.at[s, y2, lin["qa"]], Y_Q2A)
        arrived(amps.at[s, y2, lin["qb"]], Y_Q2B)
        arrived(amps.at[s, y2, lin["pa"]], R_NRA)
        arrived(amps.at[s, y2, lin["pb"]], L_NRB)
        consume(lin_left, wlin, amps, y2)

        coups[s, r] = acc[...].astype(BF16)
        block = [coups.at[s, r, half_a], coups.at[s, r, half_b]]
        final = (mirror.at[s, core], M_0 + core)

        def forward(src, key, target, dev):
            message(src, target[0], key, dev, target[1]).start()

        @pl.when(opposite)
        def _():
            first = (transit.at[s, 0], X_0)
            forward(block[0], M_0, first, place(x + 1, z, lo, hi, core))
            forward(block[1], M_1, first, place(x - 1, z, lo, hi, core))


        open_q(coups, COL)
        open_p(coups, COL)

        @pl.when(beside)
        def _():
            crossing = ahead // 2
            forward(
                block[1], M_1, (transit.at[s, crossing], X_0 + crossing),
                place(x, x, hi, lo, core),
            )
            forward(block[0], M_0, final, place(z, x, hi, lo, 0))

        for a in range(2):
            @pl.when(mout[a])
            def _():
                forward(block[a], M_0 + a, final, place(x, z, hi, lo, a))

            @pl.when(mself[a])
            def _():
                mirror[s, a] = coups[s, r, a * V:(a + 1) * V, :]

        for a in range(2):
            at = slice(a * V, (a + 1) * V)
            linear = coul[c, at, :].astype(F32) + coupling * coups[s, r, at, :].astype(F32)
            base[at, :] = damping * state[at, :] - linear * inv[at, :]
        arrived(rows.at[s, hm, lin["p"]], ZR_HP)
        send(rows.at[s, hm, half_a], ZR_HA, to_zr)
        arrived(rows.at[s, hp, lin["p"]], ZL_HP)
        arrived(rows.at[s, hp, lin["q"]], ZL_HQ)
        send(rows.at[s, hp, half_b], ZL_HB, to_zl)
        @pl.when(beside)
        def _():
            arrived(transit.at[s, 0], X_0)
            forward(
                transit.at[s, 0], X_0, (transit.at[s, 1], X_1), place(x, z + 2, hi, lo, core)
            )

        relay_q(coups, COL)
        arrived(rows.at[s, hm, lin["q"]], ZR_HQ)
        send(rows.at[s, hm], S_HM, to_s)
        send(rows.at[s, hp], S_HP, to_s)
        relay_n(coups, COL)
        @pl.when(diagonal)
        def _():
            for at, px in ((0, x + 1), (1, x - 1)):
                arrived(transit.at[s, at], X_0 + at)
                forward(transit.at[s, at], X_0 + at, final, place(px, z, lo, hi, 1))

        arrived(rows.at[s, h2, half_a], ZR_HA)
        send(rows.at[s, h2, half_a], S_H2A, to_s)
        @pl.when(beside)
        def _():
            arrived(transit.at[s, 1], X_1)
            forward(transit.at[s, 1], X_1, final, place(x - step, z, lo, hi, ahead % 3))

        relay_p(coups, COL)
        arrived(rows.at[s, h2, half_b], ZL_HB)
        send(rows.at[s, h2, half_b], S_H2B, to_s)
        relay_q2(coups, COL)
        relay_nn(coups, COL)
        arrived(coups.at[s, ry, quad["q"]], COL + Y_Q)
        for own, key in (
            (c, S_O), (ch, S_H), (cm, S_M), (cp, S_P), (hm, S_HM), (hp, S_HP), (c2, S_2),
        ):
            arrived(rows.at[s, flip(own, 1)], key)
        arrived(rows.at[s, flip(h2, 1), half_a], S_H2A)
        arrived(rows.at[s, flip(h2, 1), half_b], S_H2B)
        consume(quad_left, wquad, coups, r, first=True)
        consume(quad_left, wquad, coups, rm)
        consume(quad_left, wquad, coups, rp)
        consume(quad_left, wquad, coups, ry)
        arrived(coups.at[s, ym, quad["q"]], COL + Y_QM)
        consume(quad_left, wquad, coups, ym)
        arrived(coups.at[s, yp, quad["q"]], COL + Y_QP)
        consume(quad_left, wquad, coups, yp)
        arrived(coups.at[s, r2, quad["pa"]], COL + R_PA)
        arrived(coups.at[s, r2, quad["pb"]], COL + L_PB)
        consume(quad_left, wquad, coups, r2)
        for a in range(2):
            @pl.when(jnp.logical_not(mself[a]))
            def _():
                arrived(mirror.at[s, a], M_0 + a)

            at = slice(a * V, (a + 1) * V)
            flipped = mirror[s, a].astype(F32).T
            base[at, :] -= coupling * flipped * inv[at, :]
        arrived(coups.at[s, y2, quad["qa"]], COL + Y_Q2A)
        arrived(coups.at[s, y2, quad["qb"]], COL + Y_Q2B)
        arrived(coups.at[s, y2, quad["pa"]], COL + R_NRA)
        arrived(coups.at[s, y2, quad["pb"]], COL + L_NRB)
        consume(quad_left, wquad, coups, y2)
        state[...] = base[...] - (coupling * coupling) * acc[...] * inv[...]
        return carry

    lax.fori_loop(0, ITERS, sweep, 0)
    for a in range(2):
        out_ref[a, 0] = state[a * V:(a + 1) * V, :]
    sizes = {}
    for o, k in cuts.items():
        for keys, part in (
            ((Y_P, R_P, L_P), "p"),
            ((Y_Q, Y_QM, Y_QP, R_Q, L_Q), "q"),
            ((Y_Q2A, Y_Q2B, R_QA, L_QB), "qa"),
            ((R_NA, R_NB, R_PA, R_NRA, L_NB, L_NA, L_PB, L_NRB), "pa"),
        ):
            for key in keys:
                sizes[o + key] = amps.at[0, r, k[part]]
    sizes[N_P], sizes[N_Q] = amps.at[0, r, lin["p"]], amps.at[0, r, lin["q"]]
    for part, keys in (("p", (ZR_HP, ZL_HP)), ("q", (ZR_HQ, ZL_HQ))):
        for key in keys:
            sizes[key] = rows.at[0, c, lin[part]]
    for key in (ZR_O, ZL_O, *range(S_O, S_H2A)):
        sizes[key] = rows.at[0, c]
    for key in (ZR_OA, ZR_HA, ZL_OB, ZL_HB, S_H2A, S_H2B):
        sizes[key] = rows.at[0, c, half_a]

    def drain(s, carry):
        def sent(ref, key):
            pltpu.make_async_remote_copy(
                src_ref=ref, dst_ref=ref, send_sem=send_sem.at[s, key],
                recv_sem=recv_sem.at[s, key], device_id=to_y, device_id_type=MESH,
            ).wait_send()

        for key, ref in sizes.items():
            sent(ref, key)
        for a in range(2):
            @pl.when(jnp.logical_not(mself[a]))
            def _():
                sent(mirror.at[0, a], M_0 + a)

        @pl.when(jnp.logical_not(opposite))
        def _():
            for a in range(2):
                sent(transit.at[0, a], X_0 + a)

        return carry

    lax.fori_loop(0, ITERS, drain, 0)


def on_device(
    amplitudes,
    coulomb,
    inner_list,
    inner_count,
    reader_list,
    reader_count,
    virtual_energy,
    occupied_energy,
    *,
    nrow,
    ncol,
):
    V = amplitudes.shape[2]
    slots = inner_list.shape[2]
    hbm = pl.BlockSpec(memory_space=pltpu.HBM)
    vmem = pl.BlockSpec(memory_space=pltpu.VMEM)
    return pl.pallas_call(
        functools.partial(kernel, nrow, ncol, slots, V),
        out_shape=pltpu.VMEM(amplitudes.shape, F32),
        in_specs=[hbm] * 8,
        out_specs=vmem,
        scratch_shapes=[
            pltpu.VMEM((ITERS, nrow, 2 * V, V), BF16),
            pltpu.VMEM((ITERS, nrow, 2 * V, V), BF16),
            pltpu.VMEM((ITERS, ncol, 2 * V, V), BF16),
            pltpu.VMEM((ncol, 2 * V, V), BF16),
            pltpu.VMEM((ITERS, 2, V, V), BF16),
            pltpu.VMEM((ITERS, 2, V, V), BF16),
            pltpu.VMEM((2 * V, V), F32),
            pltpu.VMEM((2 * V, V), F32),
            pltpu.VMEM((2 * V, V), F32),
            pltpu.VMEM((2 * V, V), F32),
            pltpu.SMEM((2, ncol), F32),
            pltpu.SMEM((2, ncol), F32),
            pltpu.SMEM((2, 1, slots), jnp.int32),
            pltpu.SMEM((1, 2), jnp.int32),
            pltpu.SMEM((2, slots, ncol), jnp.int32),
            pltpu.SMEM((2, ncol), jnp.int32),
            pltpu.VMEM((1, V), F32),
            pltpu.SMEM((ncol,), F32),
            pltpu.SemaphoreType.DMA((ITERS, COUNT)),
            pltpu.SemaphoreType.DMA((ITERS, COUNT)),
            pltpu.SemaphoreType.DMA((10,)),
        ],
        compiler_params=pltpu.CompilerParams(
            collective_id=0, has_side_effects=True, vmem_limit_bytes=66000000
        ),
        name="sweeps",
    )(
        amplitudes,
        coulomb,
        inner_list,
        inner_count.T,
        reader_list.transpose(0, 2, 1),
        reader_count,
        virtual_energy.reshape(1, V),
        occupied_energy,
    )


def solution(mesh):
    return jax.shard_map(
        functools.partial(on_device, nrow=mesh.shape["row"], ncol=mesh.shape["col"]),
        mesh=mesh,
        in_specs=(
            P("row", "col", None, None),
            P("row", None, None, None),
            P("row", "col", None),
            P("row", "col"),
            P("row", None, None),
            P("row", None),
            P(),
            P(),
        ),
        out_specs=P("row", "col", None, None),
        check_vma=False,
    )
```
